32 devices in a mesh: groups: 2 (over y), chan: 4 (over z), tile: 2 (over x), rep: 2 (over core).
Axes of the slice: x: 2, y: 2, z: 4, core: 2. Of those that a mesh axis runs over, the one named last changes fastest.
Arguments:
- generator: float32 [8, 4, 512, 512], P(('groups', 'chan'), ('tile', 'rep')), parts along dimension 0, may hold values from -1.2 to 1.2
- hamiltonian: float32 [8, 4, 512, 512], P(('groups', 'chan'), ('tile', 'rep')), parts along dimension 0, may hold values from -1.2 to 1.2
- pair_weights: float32 [8, 4, 512], P(('groups', 'chan'), ('tile', 'rep')), parts along dimension 0, may hold values from -1 to 1
- cross_weights: float32 [8, 4, 3, 512], P(('groups', 'chan'), ('tile', 'rep')), parts along dimension 0, may hold values from -1 to 1
- recoupling: float32 [8, 16, 16], replicated, may hold values from -1.5 to 1.5
- cross_owner: int32 [8, 4], P('groups', ('tile', 'rep')), parts along dimension 0, may hold values from 0 to 3, as said below
- tile_order: int32 [8, 4, 16], P(('groups', 'chan'), ('tile', 'rep')), parts along dimension 0, may hold values from 0 to 15, each once within a row
- recoupling_index: int32 [8, 4], P('groups', ('tile', 'rep')), parts along dimension 0, may hold values from 0 to 7
Outputs:
- commutator: float32 [8, 4, 512, 512], P(('groups', 'chan'), ('tile', 'rep')), parts along dimension 0
The draws below stay inside these ranges and needn't reach their ends.
There are 2 independent parts, one for each index of `groups`. The reference program is written for one: setup_inputs(seed, part) draws one part's arguments, and reference() takes and returns one part's arrays. A program takes and returns all parts, laid end to end along the dimension named above; an argument that names none is the same for every part. Nothing has to cross between parts.
Inputs may be any that keep to these rules, and one draw needn't show every extreme that they name: `cross_owner`: in every column no owner hosts more than 3 cross-coupled channels, and one owner hosts exactly 3. `tile_order`: each channel's list names every one of its tiles once.
All inputs are finite; a program needn't handle non-finite values.
Results may differ from the reference program's by a relative error of at most 0.0003.
Values sent between devices are 32-bit elements; how exact they have to be, the bound alone decides.
No kernel may reach another device: no remote copies, remote signals or barrier semaphores. Data moves between devices by JAX's collectives and lax.ppermute only.
A program may use at most 64 MiB of HBM per device.

```python
import math
import jax
import jax.numpy as jnp
from jax import lax

M = 512
TS = 128
GMAX = 3
NSIX = 8
TILES = 16
KCH = 4
COLS = 4


def draw_cross_owner(key, part):

    def one_column(column_key):
        heavy_key, order_key, shuffle_key = jax.random.split(column_key, 3)
        heavy = jax.random.randint(heavy_key, (), 0, KCH).astype(jnp.int32)
        shuffled = jax.random.permutation(order_key, (KCH - 1) * GMAX)
        others = (shuffled[:KCH - GMAX] // GMAX).astype(jnp.int32)
        others = others + (others >= heavy).astype(jnp.int32)
        owners = jnp.concatenate([jnp.full((GMAX,), heavy, dtype=jnp.int32), others])
        return jax.random.permutation(shuffle_key, owners).astype(jnp.int32)
    column_keys = jax.random.split(jax.random.fold_in(key, 17), COLS)
    return jnp.transpose(jax.vmap(one_column)(column_keys)).astype(jnp.int32)


def touch_ends(drawn, key, least, top_value):
    longest = drawn.shape.index(max(drawn.shape))
    spots = []
    for shift in (0, 1):
        where = [jax.random.randint(jax.random.fold_in(key, axis), (), 0, length) for axis, length in enumerate(drawn.shape)]
        where[longest] = (where[longest] + shift) % drawn.shape[longest]
        spots.append(tuple(where))
    return drawn.at[spots[0]].set(least).at[spots[1]].set(top_value)


def shard_levels(key, dims, shards, low, largest):
    def one(dim, shards_of):
        steps = jax.random.uniform(jax.random.fold_in(jax.random.fold_in(key, 6), dim), (shards_of,), jnp.float32, low / len(shards), largest / len(shards))
        return jnp.repeat(jnp.exp(steps), dims[dim] // shards_of).reshape((-1,) + (1,) * (len(dims) - dim - 1))

    loudness = one(*shards[0])
    for cut in shards[1:]:
        loudness = loudness * one(*cut)
    return loudness


def bell_draw(stream_key, shape, scale, most, cuts=(), held_as=jnp.bfloat16):
    drawn = scale * jax.random.normal(stream_key, shape, jnp.float32)
    if cuts:
        drawn = drawn * shard_levels(stream_key, shape, cuts, -0.22, 0.18)
    return jnp.clip(drawn, -most, most).astype(held_as)


def setup_inputs(seed: int = 0, part: int = 0) -> dict:
    streams_of = jax.random.split(jax.random.key(seed), 9)
    part_splits = jax.random.split(jax.random.fold_in(streams_of[8], part), 9)
    generator = bell_draw(part_splits[0], (KCH, COLS, M, M), 0.2, 1.2, ((0, 4), (1, 4)), jnp.float32)
    hamiltonian = bell_draw(part_splits[1], (KCH, COLS, M, M), 0.2, 1.2, ((0, 4), (1, 4)), jnp.float32)
    pair_weights = jnp.clip(jax.random.uniform(part_splits[2], (KCH, COLS, M), jnp.float32, -1.0, 1.0) * shard_levels(part_splits[2], (KCH, COLS, M), ((0, 4), (1, 4)), -0.4, 0.0), -1.0, 1.0)
    cross_weights = jnp.clip(jax.random.uniform(part_splits[3], (KCH, COLS, GMAX, M), jnp.float32, -1.0, 1.0) * shard_levels(part_splits[3], (KCH, COLS, GMAX, M), ((0, 4), (1, 4)), -0.4, 0.0), -1.0, 1.0)
    recoupling = bell_draw(streams_of[4], (NSIX, TILES, TILES), 0.25, 1.5, (), jnp.float32)
    cross_owner = draw_cross_owner(jax.random.fold_in(jax.random.fold_in(streams_of[8], part), 71), part)
    tile_order = jax.vmap(lambda own: jax.random.permutation(own, TILES))(jax.random.split(part_splits[6], KCH * COLS)).reshape((KCH, COLS, TILES)).astype(jnp.int32)
    recoupling_index = touch_ends(jax.random.randint(part_splits[7], (KCH, COLS), 0, NSIX), jax.random.fold_in(part_splits[7], 1), 0, NSIX - 1).astype(jnp.int32)
    return {"generator": generator, "hamiltonian": hamiltonian, "pair_weights": pair_weights, "cross_weights": cross_weights, "recoupling": recoupling, "cross_owner": cross_owner, "tile_order": tile_order, "recoupling_index": recoupling_index}


highest = lax.Precision.HIGHEST

def to_tiles(matrix, tile_size):
    leading = matrix.shape[:-2]
    blocks = matrix.shape[-1] // tile_size
    shaped = matrix.reshape(leading + (blocks, tile_size, blocks, tile_size))
    shaped = jnp.swapaxes(shaped, -3, -2)
    return shaped.reshape(leading + (blocks * blocks, tile_size, tile_size))

def from_tiles(pieces, tile_size):
    leading = pieces.shape[:-3]
    blocks = math.isqrt(pieces.shape[-3])
    shaped = pieces.reshape(leading + (blocks, blocks, tile_size, tile_size))
    shaped = jnp.swapaxes(shaped, -3, -2)
    return shaped.reshape(leading + (blocks * tile_size, blocks * tile_size))

def bracket(left_matrix, right_matrix, weights):
    scaled = weights[..., None, :]
    left_term = jnp.matmul(left_matrix * scaled, right_matrix, precision=highest)
    right_term = jnp.matmul(right_matrix * scaled, left_matrix, precision=highest)
    return left_term - right_term

def reference(generator, hamiltonian, pair_weights, cross_weights, recoupling, cross_owner, tile_order, recoupling_index):
    channels = generator.shape[0]
    column_count = generator.shape[1]
    spread = TILES // channels
    chan_range = jnp.arange(channels, dtype=jnp.int32)
    positions = jnp.arange(TILES, dtype=jnp.int32)
    source = jnp.broadcast_to(positions[None, :] % channels, (channels, TILES))
    ordinal = chan_range[:, None] * spread + positions[None, :] // channels
    earlier = chan_range[None, :] < chan_range[:, None]

    def column(column_at):
        generator_column = lax.dynamic_index_in_dim(generator, column_at, 1, keepdims=False)
        hamilton_column = lax.dynamic_index_in_dim(hamiltonian, column_at, 1, keepdims=False)
        pair_column = lax.dynamic_index_in_dim(pair_weights, column_at, 1, keepdims=False)
        cross_column = lax.dynamic_index_in_dim(cross_weights, column_at, 1, keepdims=False)
        owners = lax.dynamic_index_in_dim(cross_owner, column_at, 1, keepdims=False)
        order_column = lax.dynamic_index_in_dim(tile_order, column_at, 1, keepdims=False)
        mixer_column = lax.dynamic_index_in_dim(recoupling_index, column_at, 1, keepdims=False)
        chosen = order_column[source, ordinal]
        generator_tiles = to_tiles(generator_column, TS)
        hamilton_tiles = to_tiles(hamilton_column, TS)
        generator_cross = generator_tiles[source, chosen]
        hamilton_cross = hamilton_tiles[source, chosen]
        mixers = recoupling[mixer_column]
        generator_mixed = jnp.einsum('gji,gixy->gjxy', mixers, generator_cross, precision=highest)
        hamilton_mixed = jnp.einsum('gji,gixy->gjxy', mixers, hamilton_cross, precision=highest)
        same_owner = owners[:, None] == owners[None, :]
        slot_of = lax.optimization_barrier(jnp.sum((same_owner & earlier).astype(jnp.int32), axis=1))
        weights_cross = cross_column[owners, slot_of]
        product = bracket(from_tiles(generator_mixed, TS), from_tiles(hamilton_mixed, TS), weights_cross)
        returned = jnp.einsum('gji,gjxy->gixy', mixers, to_tiles(product, TS), precision=highest)
        placed = jnp.zeros_like(generator_tiles).at[source, chosen].set(returned)
        direct = bracket(generator_column, hamilton_column, pair_column)
        summed = direct + from_tiles(placed, TS)
        return 0.5 * (summed + jnp.swapaxes(summed, -1, -2))
    stacked = lax.map(column, jnp.arange(column_count, dtype=jnp.int32))
    return jnp.moveaxis(stacked, 0, 1)
```

```python
import math

import jax
import jax.numpy as jnp
from jax import lax
from jax.sharding import PartitionSpec as P

TS = 128


highest = lax.Precision.HIGHEST


def to_tiles(matrix, tile_size):
    leading = matrix.shape[:-2]
    blocks = matrix.shape[-1] // tile_size
    shaped = matrix.reshape(leading + (blocks, tile_size, blocks, tile_size))
    shaped = jnp.swapaxes(shaped, -3, -2)
    return shaped.reshape(leading + (blocks * blocks, tile_size, tile_size))


def from_tiles(pieces, tile_size):
    leading = pieces.shape[:-3]
    blocks = math.isqrt(pieces.shape[-3])
    shaped = pieces.reshape(leading + (blocks, blocks, tile_size, tile_size))
    shaped = jnp.swapaxes(shaped, -3, -2)
    return shaped.reshape(leading + (blocks * tile_size, blocks * tile_size))


def bracket(left_matrix, right_matrix, weights):
    scaled = weights[..., None, :]
    left_term = jnp.matmul(left_matrix * scaled, right_matrix, precision=highest)
    right_term = jnp.matmul(right_matrix * scaled, left_matrix, precision=highest)
    return left_term - right_term


def body(
    generator,
    hamiltonian,
    pair_weights,
    cross_weights,
    recoupling,
    cross_owner,
    tile_order,
    recoupling_index,
):
    channels = cross_owner.shape[0]
    tile_count = tile_order.shape[-1]
    spread = tile_count // channels
    capacity = cross_weights.shape[2]
    me = lax.axis_index("chan")
    chan_range = jnp.arange(channels, dtype=jnp.int32)
    tile_range = jnp.arange(tile_count, dtype=jnp.int32)

    order = tile_order[0, 0]
    owners = cross_owner[:, 0]
    earlier = chan_range[None, :] < chan_range[:, None]
    same_owner = owners[:, None] == owners[None, :]
    slot_of = jnp.sum((same_owner & earlier).astype(jnp.int32), axis=1)

    generator_tiles = to_tiles(generator[0, 0], TS)
    hamilton_tiles = to_tiles(hamiltonian[0, 0], TS)
    send = jnp.stack([generator_tiles[order], hamilton_tiles[order]], axis=1)
    send = send.reshape(channels, spread, 2, TS, TS)
    got = lax.all_to_all(send, "chan", 0, 0, tiled=True)

    weight_send = cross_weights[0, 0][jnp.clip(slot_of, 0, capacity - 1)]
    weight_got = lax.all_to_all(weight_send, "chan", 0, 0, tiled=True)
    weights_cross = weight_got[owners[me]]

    cross = jnp.swapaxes(got, 0, 1).reshape(tile_count, 2, TS, TS)
    mixer = recoupling[recoupling_index[me, 0]]
    generator_mixed = jnp.einsum("ji,ixy->jxy", mixer, cross[:, 0], precision=highest)
    hamilton_mixed = jnp.einsum("ji,ixy->jxy", mixer, cross[:, 1], precision=highest)
    product = bracket(
        from_tiles(generator_mixed, TS), from_tiles(hamilton_mixed, TS), weights_cross
    )
    back = jnp.einsum("ji,jxy->ixy", mixer, to_tiles(product, TS), precision=highest)
    back = jnp.swapaxes(back.reshape(spread, channels, TS, TS), 0, 1)
    home = lax.all_to_all(back, "chan", 0, 0, tiled=True)
    inverse = jnp.zeros((tile_count,), jnp.int32).at[order].set(tile_range)
    returned = home.reshape(tile_count, TS, TS)[inverse]

    direct = bracket(generator[0, 0], hamiltonian[0, 0], pair_weights[0, 0])
    summed = direct + from_tiles(returned, TS)
    return (0.5 * (summed + summed.T))[None, None]


def solution(mesh):
    placed = (
        P(("groups", "chan"), ("tile", "rep"), None, None),
        P(("groups", "chan"), ("tile", "rep"), None, None),
        P(("groups", "chan"), ("tile", "rep"), None),
        P(("groups", "chan"), ("tile", "rep"), None, None),
        P(),
        P("groups", ("tile", "rep")),
        P(("groups", "chan"), ("tile", "rep"), None),
        P("groups", ("tile", "rep")),
    )
    return jax.shard_map(
        body,
        mesh=mesh,
        in_specs=placed,
        out_specs=P(("groups", "chan"), ("tile", "rep"), None, None),
        check_vma=False,
    )
```

```python
import math

import jax
import jax.numpy as jnp
from jax import lax
from jax.sharding import PartitionSpec as P

TS = 128


highest = lax.Precision.HIGHEST


def to_tiles(matrix, tile_size):
    leading = matrix.shape[:-2]
    blocks = matrix.shape[-1] // tile_size
    shaped = matrix.reshape(leading + (blocks, tile_size, blocks, tile_size))
    shaped = jnp.swapaxes(shaped, -3, -2)
    return shaped.reshape(leading + (blocks * blocks, tile_size, tile_size))


def from_tiles(pieces, tile_size):
    leading = pieces.shape[:-3]
    blocks = math.isqrt(pieces.shape[-3])
    shaped = pieces.reshape(leading + (blocks, blocks, tile_size, tile_size))
    shaped = jnp.swapaxes(shaped, -3, -2)
    return shaped.reshape(leading + (blocks * tile_size, blocks * tile_size))


def bracket(left_matrix, right_matrix, weights):
    scaled = weights[..., None, :]
    left_term = jnp.matmul(left_matrix * scaled, right_matrix, precision=highest)
    right_term = jnp.matmul(right_matrix * scaled, left_matrix, precision=highest)
    return left_term - right_term


def body(
    generator,
    hamiltonian,
    pair_weights,
    cross_weights,
    recoupling,
    cross_owner,
    tile_order,
    recoupling_index,
):
    channels = cross_owner.shape[0]
    tile_count = tile_order.shape[-1]
    spread = tile_count // channels
    capacity = cross_weights.shape[2]
    me = lax.axis_index("chan")
    chan_range = jnp.arange(channels, dtype=jnp.int32)
    spread_range = jnp.arange(spread, dtype=jnp.int32)
    tile_range = jnp.arange(tile_count, dtype=jnp.int32)

    order = tile_order[0, 0]
    owners = cross_owner[:, 0]
    earlier = chan_range[None, :] < chan_range[:, None]
    same_owner = owners[:, None] == owners[None, :]
    slot_of = jnp.sum((same_owner & earlier).astype(jnp.int32), axis=1)

    dest = (me + chan_range) % channels
    source = (me - chan_range) % channels
    generator_tiles = to_tiles(generator[0, 0], TS)
    hamilton_tiles = to_tiles(hamiltonian[0, 0], TS)
    picked = order[dest[:, None] * spread + spread_range[None, :]]
    send = jnp.stack([generator_tiles[picked], hamilton_tiles[picked]], axis=2)
    weight_send = cross_weights[0, 0][jnp.clip(slot_of[dest], 0, capacity - 1)]
    got = [send[0]]
    weight_got = [weight_send[0]]
    for shift in range(1, channels):
        pairs = [(c, (c + shift) % channels) for c in range(channels)]
        tiles_in, weights_in = lax.ppermute((send[shift], weight_send[shift]), "chan", pairs)
        got.append(tiles_in)
        weight_got.append(weights_in)
    got = jnp.stack(got)
    weights_cross = jnp.stack(weight_got)[(me - owners[me]) % channels]

    mixer = recoupling[recoupling_index[me, 0]]
    column_of = (spread_range[None, :] * channels + source[:, None]).reshape(-1)
    mixer_in = mixer[:, column_of]
    cross = got.reshape(tile_count, 2, TS, TS)
    generator_mixed = jnp.einsum("ji,ixy->jxy", mixer_in, cross[:, 0], precision=highest)
    hamilton_mixed = jnp.einsum("ji,ixy->jxy", mixer_in, cross[:, 1], precision=highest)
    product = bracket(
        from_tiles(generator_mixed, TS), from_tiles(hamilton_mixed, TS), weights_cross
    )
    mixer_out = mixer[:, (spread_range[None, :] * channels + dest[:, None]).reshape(-1)]
    back = jnp.einsum("ji,jxy->ixy", mixer_out, to_tiles(product, TS), precision=highest)
    back = back.reshape(channels, spread, TS, TS)
    home = [back[0]]
    for shift in range(1, channels):
        pairs = [(c, (c + shift) % channels) for c in range(channels)]
        home.append(lax.ppermute(back[shift], "chan", pairs))
    home = jnp.stack(home)
    inverse = jnp.zeros((tile_count,), jnp.int32).at[order].set(tile_range)
    from_g = inverse // spread
    at_shift = (me - from_g) % channels
    returned = home[at_shift, inverse % spread]

    direct = bracket(generator[0, 0], hamiltonian[0, 0], pair_weights[0, 0])
    summed = direct + from_tiles(returned, TS)
    return (0.5 * (summed + summed.T))[None, None]


def solution(mesh):
    placed = (
        P(("groups", "chan"), ("tile", "rep"), None, None),
        P(("groups", "chan"), ("tile", "rep"), None, None),
        P(("groups", "chan"), ("tile", "rep"), None),
        P(("groups", "chan"), ("tile", "rep"), None, None),
        P(),
        P("groups", ("tile", "rep")),
        P(("groups", "chan"), ("tile", "rep"), None),
        P("groups", ("tile", "rep")),
    )
    return jax.shard_map(
        body,
        mesh=mesh,
        in_specs=placed,
        out_specs=P(("groups", "chan"), ("tile", "rep"), None, None),
        check_vma=False,
    )
```

```python
import math

import jax
import jax.numpy as jnp
from jax import lax
from jax.sharding import PartitionSpec as P
from jax.experimental import pallas as pl
from jax.experimental.pallas import tpu as pltpu

TS = 128


highest = lax.Precision.HIGHEST


def to_tiles(matrix, tile_size):
    leading = matrix.shape[:-2]
    blocks = matrix.shape[-1] // tile_size
    shaped = matrix.reshape(leading + (blocks, tile_size, blocks, tile_size))
    shaped = jnp.swapaxes(shaped, -3, -2)
    return shaped.reshape(leading + (blocks * blocks, tile_size, tile_size))


def from_tiles(pieces, tile_size):
    leading = pieces.shape[:-3]
    blocks = math.isqrt(pieces.shape[-3])
    shaped = pieces.reshape(leading + (blocks, blocks, tile_size, tile_size))
    shaped = jnp.swapaxes(shaped, -3, -2)
    return shaped.reshape(leading + (blocks * tile_size, blocks * tile_size))


def bracket(left_matrix, right_matrix, weights):
    scaled = weights[..., None, :]
    left_term = jnp.matmul(left_matrix * scaled, right_matrix, precision=highest)
    right_term = jnp.matmul(right_matrix * scaled, left_matrix, precision=highest)
    return left_term - right_term


def build_sends(picked, weight_slot, generator, hamiltonian, weight_rows, channels, spread):
    blocks = generator.shape[-1] // TS
    rows = 2 * spread * TS + weight_rows.shape[1]

    def kernel(picked_ref, slot_ref, gen_ref, ham_ref, weight_ref, *rest):
        outs, sems = rest[:channels], rest[channels]
        copies = []
        for s in range(channels):
            for r in range(spread):
                tile = picked_ref[s * spread + r]
                top = pl.multiple_of((tile // blocks) * TS, TS)
                left = pl.multiple_of((tile % blocks) * TS, TS)
                for m, src in enumerate((gen_ref, ham_ref)):
                    copies.append(pltpu.make_async_copy(
                        src.at[pl.ds(top, TS), pl.ds(left, TS)],
                        outs[s].at[pl.ds((2 * r + m) * TS, TS), :],
                        sems.at[len(copies)],
                    ))
            copies.append(pltpu.make_async_copy(
                weight_ref.at[slot_ref[s]],
                outs[s].at[pl.ds(2 * spread * TS, weight_rows.shape[1]), :],
                sems.at[len(copies)],
            ))
        for copy in copies:
            copy.start()
        for copy in copies:
            copy.wait()

    count = channels * (2 * spread + 1)
    return pl.pallas_call(
        kernel,
        grid_spec=pltpu.PrefetchScalarGridSpec(
            num_scalar_prefetch=2,
            grid=(1,),
            in_specs=[pl.BlockSpec(memory_space=pl.ANY)] * 3,
            out_specs=[pl.BlockSpec(memory_space=pl.ANY)] * channels,
            scratch_shapes=[pltpu.SemaphoreType.DMA((count,))],
        ),
        out_shape=[jax.ShapeDtypeStruct((rows, TS), jnp.float32)] * channels,
    )(picked, weight_slot, generator, hamiltonian, weight_rows)


def finish(direct, home, place):
    size = direct.shape[-1]
    blocks = size // TS
    spread = home[0].shape[0]

    def kernel(place_ref, direct_ref, *rest):
        pieces, out_ref = rest[:-1], rest[-1]
        for a in range(blocks):
            for b in range(blocks):
                out_ref[a * TS:(a + 1) * TS, b * TS:(b + 1) * TS] = 0.5 * (
                    direct_ref[a * TS:(a + 1) * TS, b * TS:(b + 1) * TS]
                    + direct_ref[b * TS:(b + 1) * TS, a * TS:(a + 1) * TS].T
                )
        for s, piece in enumerate(pieces):
            for r in range(spread):
                tile = place_ref[s * spread + r]
                top = pl.multiple_of((tile // blocks) * TS, TS)
                left = pl.multiple_of((tile % blocks) * TS, TS)
                value = 0.5 * piece[r]
                out_ref[pl.ds(top, TS), pl.ds(left, TS)] += value
                out_ref[pl.ds(left, TS), pl.ds(top, TS)] += value.T

    whole = pl.BlockSpec(memory_space=pltpu.VMEM)
    return pl.pallas_call(
        kernel,
        grid_spec=pltpu.PrefetchScalarGridSpec(
            num_scalar_prefetch=1,
            grid=(1,),
            in_specs=[whole] * (1 + len(home)),
            out_specs=whole,
        ),
        out_shape=jax.ShapeDtypeStruct((size, size), jnp.float32),
    )(place, direct, *home)


def body(
    generator,
    hamiltonian,
    pair_weights,
    cross_weights,
    recoupling,
    cross_owner,
    tile_order,
    recoupling_index,
):
    channels = cross_owner.shape[0]
    tile_count = tile_order.shape[-1]
    spread = tile_count // channels
    capacity = cross_weights.shape[2]
    size = generator.shape[-1]
    me = lax.axis_index("chan")
    chan_range = jnp.arange(channels, dtype=jnp.int32)
    spread_range = jnp.arange(spread, dtype=jnp.int32)

    order = tile_order[0, 0]
    owners = cross_owner[:, 0]
    earlier = chan_range[None, :] < chan_range[:, None]
    same_owner = owners[:, None] == owners[None, :]
    slot_of = jnp.sum((same_owner & earlier).astype(jnp.int32), axis=1)

    dest = (me + chan_range) % channels
    source = (me - chan_range) % channels
    picked = order[(dest[:, None] * spread + spread_range[None, :]).reshape(-1)]
    weight_slot = jnp.clip(slot_of[dest], 0, capacity - 1)
    weight_rows = cross_weights[0, 0].reshape(capacity, size // TS, TS)
    sends = build_sends(
        picked, weight_slot, generator[0, 0], hamiltonian[0, 0], weight_rows, channels, spread
    )
    got = [sends[0]]
    for shift in range(1, channels):
        pairs = [(c, (c + shift) % channels) for c in range(channels)]
        got.append(lax.ppermute(sends[shift], "chan", pairs))
    got = jnp.stack(got)
    tiles_got = got[:, : 2 * spread * TS].reshape(channels, spread, 2, TS, TS)
    weights_cross = got[(me - owners[me]) % channels, 2 * spread * TS :].reshape(-1)

    mixer = recoupling[recoupling_index[me, 0]]
    column_of = (spread_range[None, :] * channels + source[:, None]).reshape(-1)
    mixer_in = mixer[:, column_of]
    cross = tiles_got.reshape(tile_count, 2, TS, TS)
    generator_mixed = jnp.einsum("ji,ixy->jxy", mixer_in, cross[:, 0], precision=highest)
    hamilton_mixed = jnp.einsum("ji,ixy->jxy", mixer_in, cross[:, 1], precision=highest)
    product = bracket(
        from_tiles(generator_mixed, TS), from_tiles(hamilton_mixed, TS), weights_cross
    )
    mixer_out = mixer[:, (spread_range[None, :] * channels + dest[:, None]).reshape(-1)]
    back = jnp.einsum("ji,jxy->ixy", mixer_out, to_tiles(product, TS), precision=highest)
    back = back.reshape(channels, spread, TS, TS)
    home = [back[0]]
    for shift in range(1, channels):
        pairs = [(c, (c + shift) % channels) for c in range(channels)]
        home.append(lax.ppermute(back[shift], "chan", pairs))
    place = order[(source[:, None] * spread + spread_range[None, :]).reshape(-1)]

    direct = bracket(generator[0, 0], hamiltonian[0, 0], pair_weights[0, 0])
    return finish(direct, home, place)[None, None]


def solution(mesh):
    placed = (
        P(("groups", "chan"), ("tile", "rep"), None, None),
        P(("groups", "chan"), ("tile", "rep"), None, None),
        P(("groups", "chan"), ("tile", "rep"), None),
        P(("groups", "chan"), ("tile", "rep"), None, None),
        P(),
        P("groups", ("tile", "rep")),
        P(("groups", "chan"), ("tile", "rep"), None),
        P("groups", ("tile", "rep")),
    )
    return jax.shard_map(
        body,
        mesh=mesh,
        in_specs=placed,
        out_specs=P(("groups", "chan"), ("tile", "rep"), None, None),
        check_vma=False,
    )
```

```python
import math

import jax
import jax.numpy as jnp
from jax import lax
from jax.sharding import PartitionSpec as P
from jax.experimental import pallas as pl
from jax.experimental.pallas import tpu as pltpu

TS = 128


highest = lax.Precision.HIGHEST


def to_tiles(matrix, tile_size):
    leading = matrix.shape[:-2]
    blocks = matrix.shape[-1] // tile_size
    shaped = matrix.reshape(leading + (blocks, tile_size, blocks, tile_size))
    shaped = jnp.swapaxes(shaped, -3, -2)
    return shaped.reshape(leading + (blocks * blocks, tile_size, tile_size))


def from_tiles(pieces, tile_size):
    leading = pieces.shape[:-3]
    blocks = math.isqrt(pieces.shape[-3])
    shaped = pieces.reshape(leading + (blocks, blocks, tile_size, tile_size))
    shaped = jnp.swapaxes(shaped, -3, -2)
    return shaped.reshape(leading + (blocks * tile_size, blocks * tile_size))


def bracket(left_matrix, right_matrix, weights):
    scaled = weights[..., None, :]
    left_term = jnp.matmul(left_matrix * scaled, right_matrix, precision=highest)
    right_term = jnp.matmul(right_matrix * scaled, left_matrix, precision=highest)
    return left_term - right_term


def build_sends(picked, weight_slot, generator, hamiltonian, weight_rows, channels, spread):
    blocks = generator.shape[-1] // TS
    rows = 2 * spread * TS + weight_rows.shape[1]

    def kernel(picked_ref, slot_ref, gen_ref, ham_ref, weight_ref, *outs):
        for s in range(channels):
            for r in range(spread):
                tile = picked_ref[s * spread + r]
                top = pl.multiple_of((tile // blocks) * TS, TS)
                left = pl.multiple_of((tile % blocks) * TS, TS)
                for m, src in enumerate((gen_ref, ham_ref)):
                    outs[s][(2 * r + m) * TS:(2 * r + m + 1) * TS, :] = src[
                        pl.ds(top, TS), pl.ds(left, TS)
                    ]
            outs[s][2 * spread * TS:, :] = weight_ref[slot_ref[s]]

    whole = pl.BlockSpec(memory_space=pltpu.VMEM)
    return pl.pallas_call(
        kernel,
        grid_spec=pltpu.PrefetchScalarGridSpec(
            num_scalar_prefetch=2,
            grid=(1,),
            in_specs=[whole] * 3,
            out_specs=[whole] * channels,
        ),
        out_shape=[jax.ShapeDtypeStruct((rows, TS), jnp.float32)] * channels,
    )(picked, weight_slot, generator, hamiltonian, weight_rows)


def finish(direct, home, place):
    size = direct.shape[-1]
    blocks = size // TS
    spread = home[0].shape[0]

    def kernel(place_ref, direct_ref, *rest):
        pieces, out_ref = rest[:-1], rest[-1]
        for a in range(blocks):
            for b in range(blocks):
                out_ref[a * TS:(a + 1) * TS, b * TS:(b + 1) * TS] = 0.5 * (
                    direct_ref[a * TS:(a + 1) * TS, b * TS:(b + 1) * TS]
                    + direct_ref[b * TS:(b + 1) * TS, a * TS:(a + 1) * TS].T
                )
        for s, piece in enumerate(pieces):
            for r in range(spread):
                tile = place_ref[s * spread + r]
                top = pl.multiple_of((tile // blocks) * TS, TS)
                left = pl.multiple_of((tile % blocks) * TS, TS)
                value = 0.5 * piece[r]
                out_ref[pl.ds(top, TS), pl.ds(left, TS)] += value
                out_ref[pl.ds(left, TS), pl.ds(top, TS)] += value.T

    whole = pl.BlockSpec(memory_space=pltpu.VMEM)
    return pl.pallas_call(
        kernel,
        grid_spec=pltpu.PrefetchScalarGridSpec(
            num_scalar_prefetch=1,
            grid=(1,),
            in_specs=[whole] * (1 + len(home)),
            out_specs=whole,
        ),
        out_shape=jax.ShapeDtypeStruct((size, size), jnp.float32),
    )(place, direct, *home)


def body(
    generator,
    hamiltonian,
    pair_weights,
    cross_weights,
    recoupling,
    cross_owner,
    tile_order,
    recoupling_index,
):
    channels = cross_owner.shape[0]
    tile_count = tile_order.shape[-1]
    spread = tile_count // channels
    capacity = cross_weights.shape[2]
    size = generator.shape[-1]
    me = lax.axis_index("chan")
    chan_range = jnp.arange(channels, dtype=jnp.int32)
    spread_range = jnp.arange(spread, dtype=jnp.int32)

    order = tile_order[0, 0]
    owners = cross_owner[:, 0]
    earlier = chan_range[None, :] < chan_range[:, None]
    same_owner = owners[:, None] == owners[None, :]
    slot_of = jnp.sum((same_owner & earlier).astype(jnp.int32), axis=1)

    dest = (me + chan_range) % channels
    source = (me - chan_range) % channels
    picked = order[(dest[:, None] * spread + spread_range[None, :]).reshape(-1)]
    weight_slot = jnp.clip(slot_of[dest], 0, capacity - 1)
    weight_rows = cross_weights[0, 0].reshape(capacity, size // TS, TS)
    sends = build_sends(
        picked, weight_slot, generator[0, 0], hamiltonian[0, 0], weight_rows, channels, spread
    )
    got = [sends[0]]
    for shift in range(1, channels):
        pairs = [(c, (c + shift) % channels) for c in range(channels)]
        got.append(lax.ppermute(sends[shift], "chan", pairs))
    got = jnp.stack(got)
    tiles_got = got[:, : 2 * spread * TS].reshape(channels, spread, 2, TS, TS)
    weights_cross = got[(me - owners[me]) % channels, 2 * spread * TS :].reshape(-1)

    mixer = recoupling[recoupling_index[me, 0]]
    column_of = (spread_range[None, :] * channels + source[:, None]).reshape(-1)
    mixer_in = mixer[:, column_of]
    cross = tiles_got.reshape(tile_count, 2, TS, TS)
    generator_mixed = jnp.einsum("ji,ixy->jxy", mixer_in, cross[:, 0], precision=highest)
    hamilton_mixed = jnp.einsum("ji,ixy->jxy", mixer_in, cross[:, 1], precision=highest)
    product = bracket(
        from_tiles(generator_mixed, TS), from_tiles(hamilton_mixed, TS), weights_cross
    )
    mixer_out = mixer[:, (spread_range[None, :] * channels + dest[:, None]).reshape(-1)]
    back = jnp.einsum("ji,jxy->ixy", mixer_out, to_tiles(product, TS), precision=highest)
    back = back.reshape(channels, spread, TS, TS)
    home = [back[0]]
    for shift in range(1, channels):
        pairs = [(c, (c + shift) % channels) for c in range(channels)]
        home.append(lax.ppermute(back[shift], "chan", pairs))
    place = order[(source[:, None] * spread + spread_range[None, :]).reshape(-1)]

    direct = bracket(generator[0, 0], hamiltonian[0, 0], pair_weights[0, 0])
    return finish(direct, home, place)[None, None]


def solution(mesh):
    placed = (
        P(("groups", "chan"), ("tile", "rep"), None, None),
        P(("groups", "chan"), ("tile", "rep"), None, None),
        P(("groups", "chan"), ("tile", "rep"), None),
        P(("groups", "chan"), ("tile", "rep"), None, None),
        P(),
        P("groups", ("tile", "rep")),
        P(("groups", "chan"), ("tile", "rep"), None),
        P("groups", ("tile", "rep")),
    )
    return jax.shard_map(
        body,
        mesh=mesh,
        in_specs=placed,
        out_specs=P(("groups", "chan"), ("tile", "rep"), None, None),
        check_vma=False,
    )
```

```python
import math

import jax
import jax.numpy as jnp
from jax import lax
from jax.sharding import PartitionSpec as P
from jax.experimental import pallas as pl
from jax.experimental.pallas import tpu as pltpu

TS = 128


highest = lax.Precision.HIGH


def to_tiles(matrix, tile_size):
    leading = matrix.shape[:-2]
    blocks = matrix.shape[-1] // tile_size
    shaped = matrix.reshape(leading + (blocks, tile_size, blocks, tile_size))
    shaped = jnp.swapaxes(shaped, -3, -2)
    return shaped.reshape(leading + (blocks * blocks, tile_size, tile_size))


def from_tiles(pieces, tile_size):
    leading = pieces.shape[:-3]
    blocks = math.isqrt(pieces.shape[-3])
    shaped = pieces.reshape(leading + (blocks, blocks, tile_size, tile_size))
    shaped = jnp.swapaxes(shaped, -3, -2)
    return shaped.reshape(leading + (blocks * tile_size, blocks * tile_size))


def bracket(left_matrix, right_matrix, weights):
    scaled = weights[..., None, :]
    left_term = jnp.matmul(left_matrix * scaled, right_matrix, precision=highest)
    right_term = jnp.matmul(right_matrix * scaled, left_matrix, precision=highest)
    return left_term - right_term


def build_sends(picked, weight_slot, generator, hamiltonian, weight_rows, channels, spread):
    blocks = generator.shape[-1] // TS
    rows = 2 * spread * TS + weight_rows.shape[1] // TS

    def kernel(picked_ref, slot_ref, gen_ref, ham_ref, weight_ref, *outs):
        for s in range(channels):
            for r in range(spread):
                tile = picked_ref[s * spread + r]
                top = pl.multiple_of((tile // blocks) * TS, TS)
                left = pl.multiple_of((tile % blocks) * TS, TS)
                for m, src in enumerate((gen_ref, ham_ref)):
                    outs[s][(2 * r + m) * TS:(2 * r + m + 1) * TS, :] = src[
                        pl.ds(top, TS), pl.ds(left, TS)
                    ]
            slot = slot_ref[s]
            for c in range(weight_ref.shape[1] // TS):
                row = 2 * spread * TS + c
                rows_here = weight_ref[:, c * TS:(c + 1) * TS]
                value = rows_here[0:1]
                for q in range(1, weight_ref.shape[0]):
                    value = jnp.where(slot == q, rows_here[q:q + 1], value)
                outs[s][row:row + 1, :] = value

    whole = pl.BlockSpec(memory_space=pltpu.VMEM)
    return pl.pallas_call(
        kernel,
        grid_spec=pltpu.PrefetchScalarGridSpec(
            num_scalar_prefetch=2,
            grid=(1,),
            in_specs=[whole] * 3,
            out_specs=[whole] * channels,
        ),
        out_shape=[jax.ShapeDtypeStruct((rows, TS), jnp.float32)] * channels,
    )(picked, weight_slot, generator, hamiltonian, weight_rows)


def finish(direct, home, place):
    size = direct.shape[-1]
    blocks = size // TS
    spread = home[0].shape[0]

    def kernel(place_ref, direct_ref, *rest):
        pieces, out_ref = rest[:-1], rest[-1]
        out_ref[...] = direct_ref[...]
        for s, piece in enumerate(pieces):
            for r in range(spread):
                tile = place_ref[s * spread + r]
                top = pl.multiple_of((tile // blocks) * TS, TS)
                left = pl.multiple_of((tile % blocks) * TS, TS)
                value = 0.5 * piece[r]
                out_ref[pl.ds(top, TS), pl.ds(left, TS)] += value
                out_ref[pl.ds(left, TS), pl.ds(top, TS)] += value.T

    whole = pl.BlockSpec(memory_space=pltpu.VMEM)
    return pl.pallas_call(
        kernel,
        grid_spec=pltpu.PrefetchScalarGridSpec(
            num_scalar_prefetch=1,
            grid=(1,),
            in_specs=[whole] * (1 + len(home)),
            out_specs=whole,
        ),
        out_shape=jax.ShapeDtypeStruct((size, size), jnp.float32),
    )(place, direct, *home)


def body(
    generator,
    hamiltonian,
    pair_weights,
    cross_weights,
    recoupling,
    cross_owner,
    tile_order,
    recoupling_index,
):
    channels = cross_owner.shape[0]
    tile_count = tile_order.shape[-1]
    spread = tile_count // channels
    capacity = cross_weights.shape[2]
    size = generator.shape[-1]
    me = lax.axis_index("chan")
    chan_range = jnp.arange(channels, dtype=jnp.int32)
    spread_range = jnp.arange(spread, dtype=jnp.int32)

    order = tile_order[0, 0]
    owners = cross_owner[:, 0]
    earlier = chan_range[None, :] < chan_range[:, None]
    same_owner = owners[:, None] == owners[None, :]
    slot_of = jnp.sum((same_owner & earlier).astype(jnp.int32), axis=1)

    dest = (me + chan_range) % channels
    source = (me - chan_range) % channels
    picked = order[(dest[:, None] * spread + spread_range[None, :]).reshape(-1)]
    weight_slot = jnp.clip(slot_of[dest], 0, capacity - 1)
    weight_rows = cross_weights[0, 0]
    sends = build_sends(
        picked, weight_slot, generator[0, 0], hamiltonian[0, 0], weight_rows, channels, spread
    )
    got = [sends[0]]
    for shift in range(1, channels):
        pairs = [(c, (c + shift) % channels) for c in range(channels)]
        got.append(lax.ppermute(sends[shift], "chan", pairs))
    got = jnp.stack(got)
    tiles_got = got[:, : 2 * spread * TS].reshape(channels, spread, 2, TS, TS)
    weights_cross = got[(me - owners[me]) % channels, 2 * spread * TS :].reshape(-1)

    mixer = recoupling[recoupling_index[me, 0]]
    column_of = (spread_range[None, :] * channels + source[:, None]).reshape(-1)
    mixer_in = mixer[:, column_of]
    cross = tiles_got.reshape(tile_count, 2, TS, TS)
    generator_mixed = jnp.einsum("ji,ixy->jxy", mixer_in, cross[:, 0], precision=highest)
    hamilton_mixed = jnp.einsum("ji,ixy->jxy", mixer_in, cross[:, 1], precision=highest)
    product = bracket(
        from_tiles(generator_mixed, TS), from_tiles(hamilton_mixed, TS), weights_cross
    )
    mixer_out = mixer[:, (spread_range[None, :] * channels + dest[:, None]).reshape(-1)]
    back = jnp.einsum("ji,jxy->ixy", mixer_out, to_tiles(product, TS), precision=highest)
    back = back.reshape(channels, spread, TS, TS)
    home = [back[0]]
    for shift in range(1, channels):
        pairs = [(c, (c + shift) % channels) for c in range(channels)]
        home.append(lax.ppermute(back[shift], "chan", pairs))
    place = order[(source[:, None] * spread + spread_range[None, :]).reshape(-1)]

    direct = bracket(generator[0, 0], hamiltonian[0, 0], pair_weights[0, 0])
    return finish(0.5 * (direct + direct.T), home, place)[None, None]


def solution(mesh):
    placed = (
        P(("groups", "chan"), ("tile", "rep"), None, None),
        P(("groups", "chan"), ("tile", "rep"), None, None),
        P(("groups", "chan"), ("tile", "rep"), None),
        P(("groups", "chan"), ("tile", "rep"), None, None),
        P(),
        P("groups", ("tile", "rep")),
        P(("groups", "chan"), ("tile", "rep"), None),
        P("groups", ("tile", "rep")),
    )
    return jax.shard_map(
        body,
        mesh=mesh,
        in_specs=placed,
        out_specs=P(("groups", "chan"), ("tile", "rep"), None, None),
        check_vma=False,
    )
```

```python
import math

import jax
import jax.numpy as jnp
from jax import lax
from jax.sharding import PartitionSpec as P
from jax.experimental import pallas as pl
from jax.experimental.pallas import tpu as pltpu

TS = 128


highest = lax.Precision.HIGH


def to_tiles(matrix, tile_size):
    leading = matrix.shape[:-2]
    blocks = matrix.shape[-1] // tile_size
    shaped = matrix.reshape(leading + (blocks, tile_size, blocks, tile_size))
    shaped = jnp.swapaxes(shaped, -3, -2)
    return shaped.reshape(leading + (blocks * blocks, tile_size, tile_size))


def from_tiles(pieces, tile_size):
    leading = pieces.shape[:-3]
    blocks = math.isqrt(pieces.shape[-3])
    shaped = pieces.reshape(leading + (blocks, blocks, tile_size, tile_size))
    shaped = jnp.swapaxes(shaped, -3, -2)
    return shaped.reshape(leading + (blocks * tile_size, blocks * tile_size))


def bracket(left_matrix, right_matrix, weights):
    scaled = weights[..., None, :]
    left_term = jnp.matmul(left_matrix * scaled, right_matrix, precision=highest)
    right_term = jnp.matmul(right_matrix * scaled, left_matrix, precision=highest)
    return left_term - right_term


def build_sends(order, owners, generator, hamiltonian, cross_weights, channels, spread):
    blocks = generator.shape[-1] // TS
    capacity, length = cross_weights.shape[-2:]
    rows = 2 * spread * TS + length // TS

    def kernel(order_ref, owner_ref, gen_ref, ham_ref, weight_ref, *outs):
        me = lax.axis_index("chan")
        for s in range(channels):
            g = (me + s) % channels
            for r in range(spread):
                tile = order_ref[g * spread + r]
                top = pl.multiple_of((tile // blocks) * TS, TS)
                left = pl.multiple_of((tile % blocks) * TS, TS)
                for m, src in enumerate((gen_ref, ham_ref)):
                    outs[s][(2 * r + m) * TS:(2 * r + m + 1) * TS, :] = src[
                        pl.ds(top, TS), pl.ds(left, TS)
                    ]
            mine = owner_ref[g]
            slot = 0
            for other in range(channels - 1):
                slot = slot + jnp.where((other < g) & (owner_ref[other] == mine), 1, 0)
            slot = jnp.minimum(slot, capacity - 1)
            for c in range(length // TS):
                row = 2 * spread * TS + c
                rows_here = weight_ref[0, 0, :, c * TS:(c + 1) * TS]
                value = rows_here[0:1]
                for q in range(1, capacity):
                    value = jnp.where(slot == q, rows_here[q:q + 1], value)
                outs[s][row:row + 1, :] = value

    whole = pl.BlockSpec(memory_space=pltpu.VMEM)
    return pl.pallas_call(
        kernel,
        grid_spec=pltpu.PrefetchScalarGridSpec(
            num_scalar_prefetch=2,
            grid=(1,),
            in_specs=[whole] * 3,
            out_specs=[whole] * channels,
        ),
        out_shape=[jax.ShapeDtypeStruct((rows, TS), jnp.float32)] * channels,
    )(order, owners, generator, hamiltonian, cross_weights)


def finish(direct, home, place):
    size = direct.shape[-1]
    blocks = size // TS
    spread = home[0].shape[0]

    def kernel(place_ref, direct_ref, *rest):
        pieces, out_ref = rest[:-1], rest[-1]
        out_ref[...] = direct_ref[...]
        for s, piece in enumerate(pieces):
            for r in range(spread):
                tile = place_ref[s * spread + r]
                top = pl.multiple_of((tile // blocks) * TS, TS)
                left = pl.multiple_of((tile % blocks) * TS, TS)
                value = 0.5 * piece[r]
                out_ref[pl.ds(top, TS), pl.ds(left, TS)] += value
                out_ref[pl.ds(left, TS), pl.ds(top, TS)] += value.T

    whole = pl.BlockSpec(memory_space=pltpu.VMEM)
    return pl.pallas_call(
        kernel,
        grid_spec=pltpu.PrefetchScalarGridSpec(
            num_scalar_prefetch=1,
            grid=(1,),
            in_specs=[whole] * (1 + len(home)),
            out_specs=whole,
        ),
        out_shape=jax.ShapeDtypeStruct((size, size), jnp.float32),
    )(place, direct, *home)


def body(
    generator,
    hamiltonian,
    pair_weights,
    cross_weights,
    recoupling,
    cross_owner,
    tile_order,
    recoupling_index,
):
    channels = cross_owner.shape[0]
    tile_count = tile_order.shape[-1]
    spread = tile_count // channels
    capacity = cross_weights.shape[2]
    size = generator.shape[-1]
    me = lax.axis_index("chan")
    chan_range = jnp.arange(channels, dtype=jnp.int32)
    spread_range = jnp.arange(spread, dtype=jnp.int32)

    order = tile_order[0, 0]
    owners = cross_owner[:, 0]

    dest = (me + chan_range) % channels
    source = (me - chan_range) % channels
    sends = build_sends(
        order, owners, generator[0, 0], hamiltonian[0, 0], cross_weights, channels, spread
    )
    got = [sends[0]]
    for shift in range(1, channels):
        pairs = [(c, (c + shift) % channels) for c in range(channels)]
        got.append(lax.ppermute(sends[shift], "chan", pairs))
    got = jnp.stack(got)
    tiles_got = got[:, : 2 * spread * TS].reshape(channels, spread, 2, TS, TS)
    weights_cross = got[(me - owners[me]) % channels, 2 * spread * TS :].reshape(-1)

    mixer = recoupling[recoupling_index[me, 0]]
    column_of = (spread_range[None, :] * channels + source[:, None]).reshape(-1)
    mixer_in = mixer[:, column_of]
    cross = tiles_got.reshape(tile_count, 2, TS, TS)
    generator_mixed = jnp.einsum("ji,ixy->jxy", mixer_in, cross[:, 0], precision=highest)
    hamilton_mixed = jnp.einsum("ji,ixy->jxy", mixer_in, cross[:, 1], precision=highest)
    product = bracket(
        from_tiles(generator_mixed, TS), from_tiles(hamilton_mixed, TS), weights_cross
    )
    mixer_out = mixer[:, (spread_range[None, :] * channels + dest[:, None]).reshape(-1)]
    back = jnp.einsum("ji,jxy->ixy", mixer_out, to_tiles(product, TS), precision=highest)
    back = back.reshape(channels, spread, TS, TS)
    home = [back[0]]
    for shift in range(1, channels):
        pairs = [(c, (c + shift) % channels) for c in range(channels)]
        home.append(lax.ppermute(back[shift], "chan", pairs))
    place = order[(source[:, None] * spread + spread_range[None, :]).reshape(-1)]

    direct = bracket(generator[0, 0], hamiltonian[0, 0], pair_weights[0, 0])
    return finish(0.5 * (direct + direct.T), home, place)[None, None]


def solution(mesh):
    placed = (
        P(("groups", "chan"), ("tile", "rep"), None, None),
        P(("groups", "chan"), ("tile", "rep"), None, None),
        P(("groups", "chan"), ("tile", "rep"), None),
        P(("groups", "chan"), ("tile", "rep"), None, None),
        P(),
        P("groups", ("tile", "rep")),
        P(("groups", "chan"), ("tile", "rep"), None),
        P("groups", ("tile", "rep")),
    )
    return jax.shard_map(
        body,
        mesh=mesh,
        in_specs=placed,
        out_specs=P(("groups", "chan"), ("tile", "rep"), None, None),
        check_vma=False,
    )
```

```python
import math

import jax
import jax.numpy as jnp
from jax import lax
from jax.sharding import PartitionSpec as P
from jax.experimental import pallas as pl
from jax.experimental.pallas import tpu as pltpu

TS = 128


highest = lax.Precision.HIGH


def to_tiles(matrix, tile_size):
    leading = matrix.shape[:-2]
    blocks = matrix.shape[-1] // tile_size
    shaped = matrix.reshape(leading + (blocks, tile_size, blocks, tile_size))
    shaped = jnp.swapaxes(shaped, -3, -2)
    return shaped.reshape(leading + (blocks * blocks, tile_size, tile_size))


def from_tiles(pieces, tile_size):
    leading = pieces.shape[:-3]
    blocks = math.isqrt(pieces.shape[-3])
    shaped = pieces.reshape(leading + (blocks, blocks, tile_size, tile_size))
    shaped = jnp.swapaxes(shaped, -3, -2)
    return shaped.reshape(leading + (blocks * tile_size, blocks * tile_size))


def bracket(left_matrix, right_matrix, weights):
    scaled = weights[..., None, :]
    left_term = jnp.matmul(left_matrix * scaled, right_matrix, precision=highest)
    right_term = jnp.matmul(right_matrix * scaled, left_matrix, precision=highest)
    return left_term - right_term


def build_sends(order, owners, generator, hamiltonian, cross_weights, channels, spread):
    blocks = generator.shape[-1] // TS
    capacity, length = cross_weights.shape[-2:]
    rows = 2 * spread * TS + length // TS

    def kernel(order_ref, owner_ref, gen_ref, ham_ref, weight_ref, *outs):
        me = lax.axis_index("chan")
        for s in range(channels):
            g = (me + s) % channels
            for r in range(spread):
                tile = order_ref[g * spread + r]
                top = pl.multiple_of((tile // blocks) * TS, TS)
                left = pl.multiple_of((tile % blocks) * TS, TS)
                for m, src in enumerate((gen_ref, ham_ref)):
                    outs[s][(2 * r + m) * TS:(2 * r + m + 1) * TS, :] = src[
                        pl.ds(top, TS), pl.ds(left, TS)
                    ]
            mine = owner_ref[g]
            slot = 0
            for other in range(channels - 1):
                slot = slot + jnp.where((other < g) & (owner_ref[other] == mine), 1, 0)
            slot = jnp.minimum(slot, capacity - 1)
            for c in range(length // TS):
                row = 2 * spread * TS + c
                rows_here = weight_ref[0, 0, :, c * TS:(c + 1) * TS]
                value = rows_here[0:1]
                for q in range(1, capacity):
                    value = jnp.where(slot == q, rows_here[q:q + 1], value)
                outs[s][row:row + 1, :] = value

    whole = pl.BlockSpec(memory_space=pltpu.VMEM)
    return pl.pallas_call(
        kernel,
        grid_spec=pltpu.PrefetchScalarGridSpec(
            num_scalar_prefetch=2,
            grid=(1,),
            in_specs=[whole] * 3,
            out_specs=[whole] * channels,
        ),
        out_shape=[jax.ShapeDtypeStruct((rows, TS), jnp.float32)] * channels,
    )(order, owners, generator, hamiltonian, cross_weights)


def finish(direct, home, place):
    size = direct.shape[-1]
    blocks = size // TS
    spread = home[0].shape[0]

    def kernel(place_ref, direct_ref, *rest):
        pieces, out_ref = rest[:-1], rest[-1]
        a = pl.program_id(0)
        out_ref[...] = direct_ref[...]
        for s, piece in enumerate(pieces):
            for r in range(spread):
                tile = place_ref[s * spread + r]
                row, col = tile // blocks, tile % blocks

                @pl.when(row == a)
                def _():
                    left = pl.multiple_of(col * TS, TS)
                    out_ref[:, pl.ds(left, TS)] += 0.5 * piece[r]

                @pl.when(col == a)
                def _():
                    left = pl.multiple_of(row * TS, TS)
                    out_ref[:, pl.ds(left, TS)] += 0.5 * piece[r].T

    band = pl.BlockSpec((TS, size), lambda a, place: (a, 0))
    whole = pl.BlockSpec((spread, TS, TS), lambda a, place: (0, 0, 0))
    return pl.pallas_call(
        kernel,
        grid_spec=pltpu.PrefetchScalarGridSpec(
            num_scalar_prefetch=1,
            grid=(blocks,),
            in_specs=[band] + [whole] * len(home),
            out_specs=band,
        ),
        out_shape=jax.ShapeDtypeStruct((size, size), jnp.float32),
    )(place, direct, *home)


def body(
    generator,
    hamiltonian,
    pair_weights,
    cross_weights,
    recoupling,
    cross_owner,
    tile_order,
    recoupling_index,
):
    channels = cross_owner.shape[0]
    tile_count = tile_order.shape[-1]
    spread = tile_count // channels
    capacity = cross_weights.shape[2]
    size = generator.shape[-1]
    me = lax.axis_index("chan")
    chan_range = jnp.arange(channels, dtype=jnp.int32)
    spread_range = jnp.arange(spread, dtype=jnp.int32)

    order = tile_order[0, 0]
    owners = cross_owner[:, 0]

    dest = (me + chan_range) % channels
    source = (me - chan_range) % channels
    sends = build_sends(
        order, owners, generator[0, 0], hamiltonian[0, 0], cross_weights, channels, spread
    )
    got = [sends[0]]
    for shift in range(1, channels):
        pairs = [(c, (c + shift) % channels) for c in range(channels)]
        got.append(lax.ppermute(sends[shift], "chan", pairs))
    got = jnp.stack(got)
    tiles_got = got[:, : 2 * spread * TS].reshape(channels, spread, 2, TS, TS)
    weights_cross = got[(me - owners[me]) % channels, 2 * spread * TS :].reshape(-1)

    mixer = recoupling[recoupling_index[me, 0]]
    column_of = (spread_range[None, :] * channels + source[:, None]).reshape(-1)
    mixer_in = mixer[:, column_of]
    cross = tiles_got.reshape(tile_count, 2, TS, TS)
    generator_mixed = jnp.einsum("ji,ixy->jxy", mixer_in, cross[:, 0], precision=highest)
    hamilton_mixed = jnp.einsum("ji,ixy->jxy", mixer_in, cross[:, 1], precision=highest)
    product = bracket(
        from_tiles(generator_mixed, TS), from_tiles(hamilton_mixed, TS), weights_cross
    )
    mixer_out = mixer[:, (spread_range[None, :] * channels + dest[:, None]).reshape(-1)]
    back = jnp.einsum("ji,jxy->ixy", mixer_out, to_tiles(product, TS), precision=highest)
    back = back.reshape(channels, spread, TS, TS)
    home = [back[0]]
    for shift in range(1, channels):
        pairs = [(c, (c + shift) % channels) for c in range(channels)]
        home.append(lax.ppermute(back[shift], "chan", pairs))
    place = order[(source[:, None] * spread + spread_range[None, :]).reshape(-1)]

    direct = bracket(generator[0, 0], hamiltonian[0, 0], pair_weights[0, 0])
    return finish(0.5 * (direct + direct.T), home, place)[None, None]


def solution(mesh):
    placed = (
        P(("groups", "chan"), ("tile", "rep"), None, None),
        P(("groups", "chan"), ("tile", "rep"), None, None),
        P(("groups", "chan"), ("tile", "rep"), None),
        P(("groups", "chan"), ("tile", "rep"), None, None),
        P(),
        P("groups", ("tile", "rep")),
        P(("groups", "chan"), ("tile", "rep"), None),
        P("groups", ("tile", "rep")),
    )
    return jax.shard_map(
        body,
        mesh=mesh,
        in_specs=placed,
        out_specs=P(("groups", "chan"), ("tile", "rep"), None, None),
        check_vma=False,
    )
```

```python
import math

import jax
import jax.numpy as jnp
from jax import lax
from jax.sharding import PartitionSpec as P
from jax.experimental import pallas as pl
from jax.experimental.pallas import tpu as pltpu

TS = 128


highest = lax.Precision.HIGH


def to_tiles(matrix, tile_size):
    leading = matrix.shape[:-2]
    blocks = matrix.shape[-1] // tile_size
    shaped = matrix.reshape(leading + (blocks, tile_size, blocks, tile_size))
    shaped = jnp.swapaxes(shaped, -3, -2)
    return shaped.reshape(leading + (blocks * blocks, tile_size, tile_size))


def from_tiles(pieces, tile_size):
    leading = pieces.shape[:-3]
    blocks = math.isqrt(pieces.shape[-3])
    shaped = pieces.reshape(leading + (blocks, blocks, tile_size, tile_size))
    shaped = jnp.swapaxes(shaped, -3, -2)
    return shaped.reshape(leading + (blocks * tile_size, blocks * tile_size))


def bracket(left_matrix, right_matrix, weights):
    scaled = weights[..., None, :]
    left_term = jnp.matmul(left_matrix * scaled, right_matrix, precision=highest)
    right_term = jnp.matmul(right_matrix * scaled, left_matrix, precision=highest)
    return left_term - right_term


def build_sends(order, owners, generator, hamiltonian, cross_weights, channels, spread):
    blocks = generator.shape[-1] // TS
    capacity, length = cross_weights.shape[-2:]
    rows = 2 * spread * TS + length // TS

    def kernel(order_ref, owner_ref, gen_ref, ham_ref, weight_ref, *outs):
        me = lax.axis_index("chan")
        for s in range(channels):
            g = (me + s) % channels
            for r in range(spread):
                tile = order_ref[g * spread + r]
                top = pl.multiple_of((tile // blocks) * TS, TS)
                left = pl.multiple_of((tile % blocks) * TS, TS)
                for m, src in enumerate((gen_ref, ham_ref)):
                    outs[s][(2 * r + m) * TS:(2 * r + m + 1) * TS, :] = src[
                        pl.ds(top, TS), pl.ds(left, TS)
                    ]
            mine = owner_ref[g]
            slot = 0
            for other in range(channels - 1):
                slot = slot + jnp.where((other < g) & (owner_ref[other] == mine), 1, 0)
            slot = jnp.minimum(slot, capacity - 1)
            for c in range(length // TS):
                row = 2 * spread * TS + c
                rows_here = weight_ref[0, 0, :, c * TS:(c + 1) * TS]
                value = rows_here[0:1]
                for q in range(1, capacity):
                    value = jnp.where(slot == q, rows_here[q:q + 1], value)
                outs[s][row:row + 1, :] = value

    whole = pl.BlockSpec(memory_space=pltpu.VMEM)
    return pl.pallas_call(
        kernel,
        grid_spec=pltpu.PrefetchScalarGridSpec(
            num_scalar_prefetch=2,
            grid=(1,),
            in_specs=[whole] * 3,
            out_specs=[whole] * channels,
        ),
        out_shape=[jax.ShapeDtypeStruct((rows, TS), jnp.float32)] * channels,
    )(order, owners, generator, hamiltonian, cross_weights)


def finish(direct, home, place):
    size = direct.shape[-1]
    blocks = size // TS
    spread = home[0].shape[0]

    def kernel(place_ref, direct_ref, *rest):
        pieces, out_ref = rest[:-1], rest[-1]
        out_ref[...] = direct_ref[...]
        for s, piece in enumerate(pieces):
            for r in range(spread):
                tile = place_ref[s * spread + r]
                top = pl.multiple_of((tile // blocks) * TS, TS)
                left = pl.multiple_of((tile % blocks) * TS, TS)
                value = 0.5 * piece[r]
                out_ref[pl.ds(top, TS), pl.ds(left, TS)] += value
                out_ref[pl.ds(left, TS), pl.ds(top, TS)] += value.T

    whole = pl.BlockSpec(memory_space=pltpu.VMEM)
    return pl.pallas_call(
        kernel,
        grid_spec=pltpu.PrefetchScalarGridSpec(
            num_scalar_prefetch=1,
            grid=(1,),
            in_specs=[whole] * (1 + len(home)),
            out_specs=whole,
        ),
        out_shape=jax.ShapeDtypeStruct((size, size), jnp.float32),
    )(place, direct, *home)


def body(
    generator,
    hamiltonian,
    pair_weights,
    cross_weights,
    recoupling,
    cross_owner,
    tile_order,
    recoupling_index,
):
    channels = cross_owner.shape[0]
    tile_count = tile_order.shape[-1]
    spread = tile_count // channels
    capacity = cross_weights.shape[2]
    size = generator.shape[-1]
    me = lax.axis_index("chan")
    chan_range = jnp.arange(channels, dtype=jnp.int32)
    spread_range = jnp.arange(spread, dtype=jnp.int32)

    order = tile_order[0, 0]
    owners = cross_owner[:, 0]

    dest = (me + chan_range) % channels
    source = (me - chan_range) % channels
    sends = build_sends(
        order, owners, generator[0, 0], hamiltonian[0, 0], cross_weights, channels, spread
    )
    got = [sends[0]]
    for shift in range(1, channels):
        pairs = [(c, (c + shift) % channels) for c in range(channels)]
        got.append(lax.ppermute(sends[shift], "chan", pairs))
    owner_shift = (me - owners[me]) % channels
    weights_cross = sum(
        jnp.where(owner_shift == shift, piece[2 * spread * TS :], 0.0)
        for shift, piece in enumerate(got)
    ).reshape(-1)

    blocks = size // TS
    mixer = recoupling[recoupling_index[me, 0]]
    mixed = []
    for m in range(2):
        total = 0.0
        for shift, piece in enumerate(got):
            columns = spread_range * channels + source[shift]
            weights_in = mixer[:, columns].reshape(blocks, blocks, spread)
            tiles_in = piece[: 2 * spread * TS].reshape(spread, 2, TS, TS)[:, m]
            total = total + jnp.einsum("abr,rxy->axby", weights_in, tiles_in, precision=highest)
        mixed.append(total.reshape(size, size))
    product = bracket(mixed[0], mixed[1], weights_cross).reshape(blocks, TS, blocks, TS)
    mixer_out = mixer[:, (spread_range[None, :] * channels + dest[:, None]).reshape(-1)]
    back = jnp.einsum(
        "abi,axby->ixy", mixer_out.reshape(blocks, blocks, -1), product, precision=highest
    )
    back = back.reshape(channels, spread, TS, TS)
    home = [back[0]]
    for shift in range(1, channels):
        pairs = [(c, (c + shift) % channels) for c in range(channels)]
        home.append(lax.ppermute(back[shift], "chan", pairs))
    place = order[(source[:, None] * spread + spread_range[None, :]).reshape(-1)]

    direct = bracket(generator[0, 0], hamiltonian[0, 0], pair_weights[0, 0])
    return finish(0.5 * (direct + direct.T), home, place)[None, None]


def solution(mesh):
    placed = (
        P(("groups", "chan"), ("tile", "rep"), None, None),
        P(("groups", "chan"), ("tile", "rep"), None, None),
        P(("groups", "chan"), ("tile", "rep"), None),
        P(("groups", "chan"), ("tile", "rep"), None, None),
        P(),
        P("groups", ("tile", "rep")),
        P(("groups", "chan"), ("tile", "rep"), None),
        P("groups", ("tile", "rep")),
    )
    return jax.shard_map(
        body,
        mesh=mesh,
        in_specs=placed,
        out_specs=P(("groups", "chan"), ("tile", "rep"), None, None),
        check_vma=False,
    )
```

```python
import math

import jax
import jax.numpy as jnp
from jax import lax
from jax.sharding import PartitionSpec as P
from jax.experimental import pallas as pl
from jax.experimental.pallas import tpu as pltpu

TS = 128


highest = lax.Precision.HIGH


def to_tiles(matrix, tile_size):
    leading = matrix.shape[:-2]
    blocks = matrix.shape[-1] // tile_size
    shaped = matrix.reshape(leading + (blocks, tile_size, blocks, tile_size))
    shaped = jnp.swapaxes(shaped, -3, -2)
    return shaped.reshape(leading + (blocks * blocks, tile_size, tile_size))


def from_tiles(pieces, tile_size):
    leading = pieces.shape[:-3]
    blocks = math.isqrt(pieces.shape[-3])
    shaped = pieces.reshape(leading + (blocks, blocks, tile_size, tile_size))
    shaped = jnp.swapaxes(shaped, -3, -2)
    return shaped.reshape(leading + (blocks * tile_size, blocks * tile_size))


def bracket(left_matrix, right_matrix, weights):
    scaled = weights[..., None, :]
    left_term = jnp.matmul(left_matrix * scaled, right_matrix, precision=highest)
    right_term = jnp.matmul(right_matrix * scaled, left_matrix, precision=highest)
    return left_term - right_term


def build_sends(order, owners, generator, hamiltonian, cross_weights, channels, spread):
    blocks = generator.shape[-1] // TS
    capacity, length = cross_weights.shape[-2:]
    rows = 2 * spread * TS + length // TS

    def kernel(order_ref, owner_ref, gen_ref, ham_ref, weight_ref, out_ref):
        for g in range(channels):
            s = g
            for r in range(spread):
                tile = order_ref[g * spread + r]
                top = pl.multiple_of((tile // blocks) * TS, TS)
                left = pl.multiple_of((tile % blocks) * TS, TS)
                for m, src in enumerate((gen_ref, ham_ref)):
                    out_ref[s, (2 * r + m) * TS:(2 * r + m + 1) * TS, :] = src[
                        pl.ds(top, TS), pl.ds(left, TS)
                    ]
            mine = owner_ref[g]
            slot = 0
            for other in range(channels - 1):
                slot = slot + jnp.where((other < g) & (owner_ref[other] == mine), 1, 0)
            slot = jnp.minimum(slot, capacity - 1)
            for c in range(length // TS):
                row = 2 * spread * TS + c
                rows_here = weight_ref[0, 0, :, c * TS:(c + 1) * TS]
                value = rows_here[0:1]
                for q in range(1, capacity):
                    value = jnp.where(slot == q, rows_here[q:q + 1], value)
                out_ref[s, row:row + 1, :] = value

    whole = pl.BlockSpec(memory_space=pltpu.VMEM)
    return pl.pallas_call(
        kernel,
        grid_spec=pltpu.PrefetchScalarGridSpec(
            num_scalar_prefetch=2,
            grid=(1,),
            in_specs=[whole] * 3,
            out_specs=whole,
        ),
        out_shape=jax.ShapeDtypeStruct((channels, rows, TS), jnp.float32),
    )(order, owners, generator, hamiltonian, cross_weights)


def finish(direct, home, place):
    size = direct.shape[-1]
    blocks = size // TS
    channels, spread = home.shape[:2]

    def kernel(place_ref, direct_ref, home_ref, out_ref):
        pieces = [home_ref.at[s] for s in range(channels)]
        out_ref[...] = direct_ref[...]
        for s, piece in enumerate(pieces):
            for r in range(spread):
                tile = place_ref[s * spread + r]
                top = pl.multiple_of((tile // blocks) * TS, TS)
                left = pl.multiple_of((tile % blocks) * TS, TS)
                value = 0.5 * piece[r]
                out_ref[pl.ds(top, TS), pl.ds(left, TS)] += value
                out_ref[pl.ds(left, TS), pl.ds(top, TS)] += value.T

    whole = pl.BlockSpec(memory_space=pltpu.VMEM)
    return pl.pallas_call(
        kernel,
        grid_spec=pltpu.PrefetchScalarGridSpec(
            num_scalar_prefetch=1,
            grid=(1,),
            in_specs=[whole] * 2,
            out_specs=whole,
        ),
        out_shape=jax.ShapeDtypeStruct((size, size), jnp.float32),
    )(place, direct, home)


def body(
    generator,
    hamiltonian,
    pair_weights,
    cross_weights,
    recoupling,
    cross_owner,
    tile_order,
    recoupling_index,
):
    channels = cross_owner.shape[0]
    tile_count = tile_order.shape[-1]
    spread = tile_count // channels
    capacity = cross_weights.shape[2]
    size = generator.shape[-1]
    me = lax.axis_index("chan")
    chan_range = jnp.arange(channels, dtype=jnp.int32)
    spread_range = jnp.arange(spread, dtype=jnp.int32)

    order = tile_order[0, 0]
    owners = cross_owner[:, 0]

    sends = build_sends(
        order, owners, generator[0, 0], hamiltonian[0, 0], cross_weights, channels, spread
    )
    got = lax.all_to_all(sends, "chan", 0, 0, tiled=True)
    tiles_got = got[:, : 2 * spread * TS].reshape(channels, spread, 2, TS, TS)
    weights_cross = got[owners[me], 2 * spread * TS :].reshape(-1)

    mixer = recoupling[recoupling_index[me, 0]]
    cross = jnp.swapaxes(tiles_got, 0, 1).reshape(tile_count, 2, TS, TS)
    generator_mixed = jnp.einsum("ji,ixy->jxy", mixer, cross[:, 0], precision=highest)
    hamilton_mixed = jnp.einsum("ji,ixy->jxy", mixer, cross[:, 1], precision=highest)
    product = bracket(
        from_tiles(generator_mixed, TS), from_tiles(hamilton_mixed, TS), weights_cross
    )
    back = jnp.einsum("ji,jxy->ixy", mixer, to_tiles(product, TS), precision=highest)
    back = jnp.swapaxes(back.reshape(spread, channels, TS, TS), 0, 1)
    home = lax.all_to_all(back, "chan", 0, 0, tiled=True)

    direct = bracket(generator[0, 0], hamiltonian[0, 0], pair_weights[0, 0])
    return finish(0.5 * (direct + direct.T), home, order)[None, None]


def solution(mesh):
    placed = (
        P(("groups", "chan"), ("tile", "rep"), None, None),
        P(("groups", "chan"), ("tile", "rep"), None, None),
        P(("groups", "chan"), ("tile", "rep"), None),
        P(("groups", "chan"), ("tile", "rep"), None, None),
        P(),
        P("groups", ("tile", "rep")),
        P(("groups", "chan"), ("tile", "rep"), None),
        P("groups", ("tile", "rep")),
    )
    return jax.shard_map(
        body,
        mesh=mesh,
        in_specs=placed,
        out_specs=P(("groups", "chan"), ("tile", "rep"), None, None),
        check_vma=False,
    )
```

```python
import math

import jax
import jax.numpy as jnp
from jax import lax
from jax.sharding import PartitionSpec as P
from jax.experimental import pallas as pl
from jax.experimental.pallas import tpu as pltpu

TS = 128


highest = lax.Precision.HIGH


def to_tiles(matrix, tile_size):
    leading = matrix.shape[:-2]
    blocks = matrix.shape[-1] // tile_size
    shaped = matrix.reshape(leading + (blocks, tile_size, blocks, tile_size))
    shaped = jnp.swapaxes(shaped, -3, -2)
    return shaped.reshape(leading + (blocks * blocks, tile_size, tile_size))


def from_tiles(pieces, tile_size):
    leading = pieces.shape[:-3]
    blocks = math.isqrt(pieces.shape[-3])
    shaped = pieces.reshape(leading + (blocks, blocks, tile_size, tile_size))
    shaped = jnp.swapaxes(shaped, -3, -2)
    return shaped.reshape(leading + (blocks * tile_size, blocks * tile_size))


def bracket(left_matrix, right_matrix, weights):
    scaled = weights[..., None, :]
    left_term = jnp.matmul(left_matrix * scaled, right_matrix, precision=highest)
    right_term = jnp.matmul(right_matrix * scaled, left_matrix, precision=highest)
    return left_term - right_term


def build_sends(order, owners, generator, hamiltonian, cross_weights, channels, spread):
    blocks = generator.shape[-1] // TS
    capacity, length = cross_weights.shape[-2:]
    rows = 2 * spread * TS + length // TS

    def kernel(order_ref, owner_ref, gen_ref, ham_ref, weight_ref, *outs):
        me = lax.axis_index("chan")
        for s in range(channels):
            g = (me + s) % channels
            for r in range(spread):
                tile = order_ref[g * spread + r]
                top = pl.multiple_of((tile // blocks) * TS, TS)
                left = pl.multiple_of((tile % blocks) * TS, TS)
                for m, src in enumerate((gen_ref, ham_ref)):
                    outs[s][(2 * r + m) * TS:(2 * r + m + 1) * TS, :] = src[
                        pl.ds(top, TS), pl.ds(left, TS)
                    ]
            mine = owner_ref[g]
            slot = 0
            for other in range(channels - 1):
                slot = slot + jnp.where((other < g) & (owner_ref[other] == mine), 1, 0)
            slot = jnp.minimum(slot, capacity - 1)
            for c in range(length // TS):
                row = 2 * spread * TS + c
                rows_here = weight_ref[0, 0, :, c * TS:(c + 1) * TS]
                value = rows_here[0:1]
                for q in range(1, capacity):
                    value = jnp.where(slot == q, rows_here[q:q + 1], value)
                outs[s][row:row + 1, :] = value

    whole = pl.BlockSpec(memory_space=pltpu.VMEM)
    return pl.pallas_call(
        kernel,
        grid_spec=pltpu.PrefetchScalarGridSpec(
            num_scalar_prefetch=2,
            grid=(1,),
            in_specs=[whole] * 3,
            out_specs=[whole] * channels,
        ),
        out_shape=[jax.ShapeDtypeStruct((rows, TS), jnp.float32)] * channels,
    )(order, owners, generator, hamiltonian, cross_weights)


def finish(direct, home, place):
    size = direct.shape[-1]
    blocks = size // TS
    channels, spread = home.shape[:2]

    def kernel(place_ref, direct_ref, home_ref, out_ref):
        pieces = [home_ref.at[s] for s in range(channels)]
        out_ref[...] = direct_ref[...]
        for s, piece in enumerate(pieces):
            for r in range(spread):
                tile = place_ref[s * spread + r]
                top = pl.multiple_of((tile // blocks) * TS, TS)
                left = pl.multiple_of((tile % blocks) * TS, TS)
                value = 0.5 * piece[r]
                out_ref[pl.ds(top, TS), pl.ds(left, TS)] += value
                out_ref[pl.ds(left, TS), pl.ds(top, TS)] += value.T

    whole = pl.BlockSpec(memory_space=pltpu.VMEM)
    return pl.pallas_call(
        kernel,
        grid_spec=pltpu.PrefetchScalarGridSpec(
            num_scalar_prefetch=1,
            grid=(1,),
            in_specs=[whole] * 2,
            out_specs=whole,
        ),
        out_shape=jax.ShapeDtypeStruct((size, size), jnp.float32),
    )(place, direct, home)


def body(
    generator,
    hamiltonian,
    pair_weights,
    cross_weights,
    recoupling,
    cross_owner,
    tile_order,
    recoupling_index,
):
    channels = cross_owner.shape[0]
    tile_count = tile_order.shape[-1]
    spread = tile_count // channels
    capacity = cross_weights.shape[2]
    size = generator.shape[-1]
    me = lax.axis_index("chan")
    chan_range = jnp.arange(channels, dtype=jnp.int32)
    spread_range = jnp.arange(spread, dtype=jnp.int32)

    order = tile_order[0, 0]
    owners = cross_owner[:, 0]

    sends = build_sends(
        order, owners, generator[0, 0], hamiltonian[0, 0], cross_weights, channels, spread
    )
    got = [sends[0]]
    for shift in range(1, channels):
        pairs = [(c, (c + shift) % channels) for c in range(channels)]
        got.append(lax.ppermute(sends[shift], "chan", pairs))
    got = jnp.stack(got)[(me - chan_range) % channels]
    tiles_got = got[:, : 2 * spread * TS].reshape(channels, spread, 2, TS, TS)
    weights_cross = got[owners[me], 2 * spread * TS :].reshape(-1)

    mixer = recoupling[recoupling_index[me, 0]]
    cross = jnp.swapaxes(tiles_got, 0, 1).reshape(tile_count, 2, TS, TS)
    generator_mixed = jnp.einsum("ji,ixy->jxy", mixer, cross[:, 0], precision=highest)
    hamilton_mixed = jnp.einsum("ji,ixy->jxy", mixer, cross[:, 1], precision=highest)
    product = bracket(
        from_tiles(generator_mixed, TS), from_tiles(hamilton_mixed, TS), weights_cross
    )
    back = jnp.einsum("ji,jxy->ixy", mixer, to_tiles(product, TS), precision=highest)
    back = jnp.swapaxes(back.reshape(spread, channels, TS, TS), 0, 1)
    home = lax.all_to_all(back, "chan", 0, 0, tiled=True)

    direct = bracket(generator[0, 0], hamiltonian[0, 0], pair_weights[0, 0])
    return finish(0.5 * (direct + direct.T), home, order)[None, None]


def solution(mesh):
    placed = (
        P(("groups", "chan"), ("tile", "rep"), None, None),
        P(("groups", "chan"), ("tile", "rep"), None, None),
        P(("groups", "chan"), ("tile", "rep"), None),
        P(("groups", "chan"), ("tile", "rep"), None, None),
        P(),
        P("groups", ("tile", "rep")),
        P(("groups", "chan"), ("tile", "rep"), None),
        P("groups", ("tile", "rep")),
    )
    return jax.shard_map(
        body,
        mesh=mesh,
        in_specs=placed,
        out_specs=P(("groups", "chan"), ("tile", "rep"), None, None),
        check_vma=False,
    )
```

```python
import math

import jax
import jax.numpy as jnp
from jax import lax
from jax.sharding import PartitionSpec as P
from jax.experimental import pallas as pl
from jax.experimental.pallas import tpu as pltpu

TS = 128


highest = lax.Precision.HIGH


def to_tiles(matrix, tile_size):
    leading = matrix.shape[:-2]
    blocks = matrix.shape[-1] // tile_size
    shaped = matrix.reshape(leading + (blocks, tile_size, blocks, tile_size))
    shaped = jnp.swapaxes(shaped, -3, -2)
    return shaped.reshape(leading + (blocks * blocks, tile_size, tile_size))


def from_tiles(pieces, tile_size):
    leading = pieces.shape[:-3]
    blocks = math.isqrt(pieces.shape[-3])
    shaped = pieces.reshape(leading + (blocks, blocks, tile_size, tile_size))
    shaped = jnp.swapaxes(shaped, -3, -2)
    return shaped.reshape(leading + (blocks * tile_size, blocks * tile_size))


def bracket(left_matrix, right_matrix, weights):
    scaled = weights[..., None, :]
    left_term = jnp.matmul(left_matrix * scaled, right_matrix, precision=highest)
    right_term = jnp.matmul(right_matrix * scaled, left_matrix, precision=highest)
    return left_term - right_term


def build_sends(order, owners, generator, hamiltonian, cross_weights, channels, spread):
    blocks = generator.shape[-1] // TS
    capacity, length = cross_weights.shape[-2:]
    rows = 2 * spread * TS + length // TS

    def kernel(order_ref, owner_ref, gen_ref, ham_ref, weight_ref, *outs):
        me = lax.axis_index("chan")
        for s in range(channels):
            g = (me + s) % channels
            for r in range(spread):
                tile = order_ref[g * spread + r]
                top = pl.multiple_of((tile // blocks) * TS, TS)
                left = pl.multiple_of((tile % blocks) * TS, TS)
                for m, src in enumerate((gen_ref, ham_ref)):
                    outs[s][(2 * r + m) * TS:(2 * r + m + 1) * TS, :] = src[
                        pl.ds(top, TS), pl.ds(left, TS)
                    ]
            mine = owner_ref[g]
            slot = 0
            for other in range(channels - 1):
                slot = slot + jnp.where((other < g) & (owner_ref[other] == mine), 1, 0)
            slot = jnp.minimum(slot, capacity - 1)
            for c in range(length // TS):
                row = 2 * spread * TS + c
                rows_here = weight_ref[0, 0, :, c * TS:(c + 1) * TS]
                value = rows_here[0:1]
                for q in range(1, capacity):
                    value = jnp.where(slot == q, rows_here[q:q + 1], value)
                outs[s][row:row + 1, :] = value

    whole = pl.BlockSpec(memory_space=pltpu.VMEM)
    return pl.pallas_call(
        kernel,
        grid_spec=pltpu.PrefetchScalarGridSpec(
            num_scalar_prefetch=2,
            grid=(1,),
            in_specs=[whole] * 3,
            out_specs=[whole] * channels,
        ),
        out_shape=[jax.ShapeDtypeStruct((rows, TS), jnp.float32)] * channels,
    )(order, owners, generator, hamiltonian, cross_weights)


def finish(direct, home, place):
    size = direct.shape[-1]
    blocks = size // TS
    spread = home[0].shape[0]

    def kernel(place_ref, direct_ref, *rest):
        pieces, out_ref = rest[:-1], rest[-1]
        out_ref[...] = direct_ref[...]
        for s, piece in enumerate(pieces):
            for r in range(spread):
                tile = place_ref[s * spread + r]
                top = pl.multiple_of((tile // blocks) * TS, TS)
                left = pl.multiple_of((tile % blocks) * TS, TS)
                value = 0.5 * piece[r]
                out_ref[pl.ds(top, TS), pl.ds(left, TS)] += value
                out_ref[pl.ds(left, TS), pl.ds(top, TS)] += value.T

    whole = pl.BlockSpec(memory_space=pltpu.VMEM)
    return pl.pallas_call(
        kernel,
        grid_spec=pltpu.PrefetchScalarGridSpec(
            num_scalar_prefetch=1,
            grid=(1,),
            in_specs=[whole] * (1 + len(home)),
            out_specs=whole,
        ),
        out_shape=jax.ShapeDtypeStruct((size, size), jnp.float32),
    )(place, direct, *home)


def three_pass_dot(left, right):
    left_high = left.astype(jnp.bfloat16)
    left_low = (left - left_high.astype(jnp.float32)).astype(jnp.bfloat16)
    right_high = right.astype(jnp.bfloat16)
    right_low = (right - right_high.astype(jnp.float32)).astype(jnp.bfloat16)
    product = jnp.dot(left_high, right_high, preferred_element_type=jnp.float32)
    product = product + jnp.dot(left_high, right_low, preferred_element_type=jnp.float32)
    return product + jnp.dot(left_low, right_high, preferred_element_type=jnp.float32)


def cross_term(pieces, mixer_in, mixer_out, owner_shift, size):
    channels = len(pieces)
    tile_count = mixer_in.shape[0]
    spread = tile_count // channels
    blocks = size // TS
    weight_at = 2 * spread * TS
    weight_rows = pieces[0].shape[0] - weight_at

    def kernel(in_ref, out_ref, shift_ref, *refs):
        got = refs[:channels]
        outs = refs[channels:2 * channels]
        left_ref, right_ref, product_ref = refs[2 * channels:]
        shift = shift_ref[0]
        weights = got[0][weight_at:weight_at + weight_rows, :]
        for s in range(1, channels):
            weights = jnp.where(shift == s, got[s][weight_at:weight_at + weight_rows, :], weights)

        for m, mixed_ref in ((0, left_ref), (1, right_ref)):
            def mix(j, carry, m=m, mixed_ref=mixed_ref):
                total = jnp.zeros((TS, TS), jnp.float32)
                for s in range(channels):
                    for r in range(spread):
                        tile = got[s][(2 * r + m) * TS:(2 * r + m + 1) * TS, :]
                        total = total + in_ref[j, s * spread + r] * tile
                top = pl.multiple_of((j // blocks) * TS, TS)
                left = pl.multiple_of((j % blocks) * TS, TS)
                mixed_ref[pl.ds(top, TS), pl.ds(left, TS)] = total
                return carry

            lax.fori_loop(0, tile_count, mix, 0)

        left = left_ref[...]
        right = right_ref[...]
        scale = jnp.concatenate([weights[b:b + 1, :] for b in range(blocks)], axis=1)
        product_ref[...] = three_pass_dot(left * scale, right) - three_pass_dot(right * scale, left)

        for s in range(channels):
            for r in range(spread):
                t = s * spread + r

                def back(j, total, t=t):
                    top = pl.multiple_of((j // blocks) * TS, TS)
                    left = pl.multiple_of((j % blocks) * TS, TS)
                    return total + out_ref[j, t] * product_ref[pl.ds(top, TS), pl.ds(left, TS)]

                outs[s][r] = lax.fori_loop(0, tile_count, back, jnp.zeros((TS, TS), jnp.float32))

    smem = pl.BlockSpec(memory_space=pltpu.SMEM)
    whole = pl.BlockSpec(memory_space=pltpu.VMEM)
    return pl.pallas_call(
        kernel,
        in_specs=[smem] * 3 + [whole] * channels,
        out_specs=[whole] * channels,
        out_shape=[jax.ShapeDtypeStruct((spread, TS, TS), jnp.float32)] * channels,
        scratch_shapes=[pltpu.VMEM((size, size), jnp.float32)] * 3,
    )(mixer_in, mixer_out, owner_shift, *pieces)


def body(
    generator,
    hamiltonian,
    pair_weights,
    cross_weights,
    recoupling,
    cross_owner,
    tile_order,
    recoupling_index,
):
    channels = cross_owner.shape[0]
    tile_count = tile_order.shape[-1]
    spread = tile_count // channels
    capacity = cross_weights.shape[2]
    size = generator.shape[-1]
    me = lax.axis_index("chan")
    chan_range = jnp.arange(channels, dtype=jnp.int32)
    spread_range = jnp.arange(spread, dtype=jnp.int32)

    order = tile_order[0, 0]
    owners = cross_owner[:, 0]

    dest = (me + chan_range) % channels
    source = (me - chan_range) % channels
    sends = build_sends(
        order, owners, generator[0, 0], hamiltonian[0, 0], cross_weights, channels, spread
    )
    got = [sends[0]]
    for shift in range(1, channels):
        pairs = [(c, (c + shift) % channels) for c in range(channels)]
        got.append(lax.ppermute(sends[shift], "chan", pairs))

    mixer = recoupling[recoupling_index[me, 0]]
    mixer_in = mixer[:, (spread_range[None, :] * channels + source[:, None]).reshape(-1)]
    mixer_out = mixer[:, (spread_range[None, :] * channels + dest[:, None]).reshape(-1)]
    owner_shift = ((me - owners[me]) % channels).reshape(1)
    back = cross_term(got, mixer_in, mixer_out, owner_shift, size)
    home = [back[0]]
    for shift in range(1, channels):
        pairs = [(c, (c + shift) % channels) for c in range(channels)]
        home.append(lax.ppermute(back[shift], "chan", pairs))
    place = order[(source[:, None] * spread + spread_range[None, :]).reshape(-1)]

    direct = bracket(generator[0, 0], hamiltonian[0, 0], pair_weights[0, 0])
    return finish(0.5 * (direct + direct.T), home, place)[None, None]


def solution(mesh):
    placed = (
        P(("groups", "chan"), ("tile", "rep"), None, None),
        P(("groups", "chan"), ("tile", "rep"), None, None),
        P(("groups", "chan"), ("tile", "rep"), None),
        P(("groups", "chan"), ("tile", "rep"), None, None),
        P(),
        P("groups", ("tile", "rep")),
        P(("groups", "chan"), ("tile", "rep"), None),
        P("groups", ("tile", "rep")),
    )
    return jax.shard_map(
        body,
        mesh=mesh,
        in_specs=placed,
        out_specs=P(("groups", "chan"), ("tile", "rep"), None, None),
        check_vma=False,
    )
```

```python
import math

import jax
import jax.numpy as jnp
from jax import lax
from jax.sharding import PartitionSpec as P
from jax.experimental import pallas as pl
from jax.experimental.pallas import tpu as pltpu

TS = 128


highest = lax.Precision.HIGH


def to_tiles(matrix, tile_size):
    leading = matrix.shape[:-2]
    blocks = matrix.shape[-1] // tile_size
    shaped = matrix.reshape(leading + (blocks, tile_size, blocks, tile_size))
    shaped = jnp.swapaxes(shaped, -3, -2)
    return shaped.reshape(leading + (blocks * blocks, tile_size, tile_size))


def from_tiles(pieces, tile_size):
    leading = pieces.shape[:-3]
    blocks = math.isqrt(pieces.shape[-3])
    shaped = pieces.reshape(leading + (blocks, blocks, tile_size, tile_size))
    shaped = jnp.swapaxes(shaped, -3, -2)
    return shaped.reshape(leading + (blocks * tile_size, blocks * tile_size))


def bracket(left_matrix, right_matrix, weights):
    scaled = weights[..., None, :]
    left_term = jnp.matmul(left_matrix * scaled, right_matrix, precision=highest)
    right_term = jnp.matmul(right_matrix * scaled, left_matrix, precision=highest)
    return left_term - right_term


def build_sends(order, owners, generator, hamiltonian, cross_weights, channels, spread):
    size = generator.shape[-1]
    blocks = size // TS
    capacity, length = cross_weights.shape[-2:]
    rows = 2 * spread * TS + length // TS

    def kernel(order_ref, owner_ref, gen_hbm, ham_hbm, weight_ref, *refs):
        outs = refs[:channels]
        gen_ref, ham_ref, bufs, in_sems, out_sems = refs[channels:]
        loads = []
        for m, (src, dst) in enumerate(((gen_hbm, gen_ref), (ham_hbm, ham_ref))):
            for b in range(blocks):
                loads.append(pltpu.make_async_copy(
                    src.at[b * TS:(b + 1) * TS, :], dst.at[b * TS:(b + 1) * TS, :], in_sems.at[m * blocks + b]
                ))
        for load in loads:
            load.start()
        for load in loads:
            load.wait()
        me = lax.axis_index("chan")
        stores = []
        for s in range(channels):
            g = (me + s) % channels
            for r in range(spread):
                tile = order_ref[g * spread + r]
                top = pl.multiple_of((tile // blocks) * TS, TS)
                left = pl.multiple_of((tile % blocks) * TS, TS)
                for m, src in enumerate((gen_ref, ham_ref)):
                    bufs[s, (2 * r + m) * TS:(2 * r + m + 1) * TS, :] = src[
                        pl.ds(top, TS), pl.ds(left, TS)
                    ]
            mine = owner_ref[g]
            slot = 0
            for other in range(channels - 1):
                slot = slot + jnp.where((other < g) & (owner_ref[other] == mine), 1, 0)
            slot = jnp.minimum(slot, capacity - 1)
            for c in range(length // TS):
                row = 2 * spread * TS + c
                rows_here = weight_ref[0, 0, :, c * TS:(c + 1) * TS]
                value = rows_here[0:1]
                for q in range(1, capacity):
                    value = jnp.where(slot == q, rows_here[q:q + 1], value)
                bufs[s, row:row + 1, :] = value
            store = pltpu.make_async_copy(bufs.at[s], outs[s], out_sems.at[s])
            store.start()
            stores.append(store)
        for store in stores:
            store.wait()

    hbm = pl.BlockSpec(memory_space=pl.ANY)
    return pl.pallas_call(
        kernel,
        grid_spec=pltpu.PrefetchScalarGridSpec(
            num_scalar_prefetch=2,
            grid=(1,),
            in_specs=[hbm, hbm, pl.BlockSpec(memory_space=pltpu.VMEM)],
            out_specs=[hbm] * channels,
            scratch_shapes=[
                pltpu.VMEM((size, size), jnp.float32),
                pltpu.VMEM((size, size), jnp.float32),
                pltpu.VMEM((channels, rows, TS), jnp.float32),
                pltpu.SemaphoreType.DMA((2 * blocks,)),
                pltpu.SemaphoreType.DMA((channels,)),
            ],
        ),
        out_shape=[jax.ShapeDtypeStruct((rows, TS), jnp.float32)] * channels,
    )(order, owners, generator, hamiltonian, cross_weights)


def finish(direct, home, place):
    size = direct.shape[-1]
    blocks = size // TS
    channels = len(home)
    spread = home[0].shape[0]

    def kernel(place_ref, direct_hbm, *refs):
        pieces_hbm = refs[:channels]
        out_hbm = refs[channels]
        work, pieces, in_sems, piece_sems, out_sems = refs[channels + 1:]
        loads = [
            pltpu.make_async_copy(
                direct_hbm.at[b * TS:(b + 1) * TS, :], work.at[b * TS:(b + 1) * TS, :], in_sems.at[b]
            )
            for b in range(blocks)
        ]
        loads += [
            pltpu.make_async_copy(pieces_hbm[s], pieces.at[s], piece_sems.at[s])
            for s in range(channels)
        ]
        for load in loads:
            load.start()
        for load in loads:
            load.wait()
        for s in range(channels):
            for r in range(spread):
                tile = place_ref[s * spread + r]
                top = pl.multiple_of((tile // blocks) * TS, TS)
                left = pl.multiple_of((tile % blocks) * TS, TS)
                value = 0.5 * pieces[s, r]
                work[pl.ds(top, TS), pl.ds(left, TS)] += value
                work[pl.ds(left, TS), pl.ds(top, TS)] += value.T
        stores = [
            pltpu.make_async_copy(
                work.at[b * TS:(b + 1) * TS, :], out_hbm.at[b * TS:(b + 1) * TS, :], out_sems.at[b]
            )
            for b in range(blocks)
        ]
        for store in stores:
            store.start()
        for store in stores:
            store.wait()

    hbm = pl.BlockSpec(memory_space=pl.ANY)
    return pl.pallas_call(
        kernel,
        grid_spec=pltpu.PrefetchScalarGridSpec(
            num_scalar_prefetch=1,
            grid=(1,),
            in_specs=[hbm] * (1 + channels),
            out_specs=hbm,
            scratch_shapes=[
                pltpu.VMEM((size, size), jnp.float32),
                pltpu.VMEM((channels, spread, TS, TS), jnp.float32),
                pltpu.SemaphoreType.DMA((blocks,)),
                pltpu.SemaphoreType.DMA((channels,)),
                pltpu.SemaphoreType.DMA((blocks,)),
            ],
        ),
        out_shape=jax.ShapeDtypeStruct((size, size), jnp.float32),
    )(place, direct, *home)


def body(
    generator,
    hamiltonian,
    pair_weights,
    cross_weights,
    recoupling,
    cross_owner,
    tile_order,
    recoupling_index,
):
    channels = cross_owner.shape[0]
    tile_count = tile_order.shape[-1]
    spread = tile_count // channels
    capacity = cross_weights.shape[2]
    size = generator.shape[-1]
    me = lax.axis_index("chan")
    chan_range = jnp.arange(channels, dtype=jnp.int32)
    spread_range = jnp.arange(spread, dtype=jnp.int32)

    order = tile_order[0, 0]
    owners = cross_owner[:, 0]

    dest = (me + chan_range) % channels
    source = (me - chan_range) % channels
    sends = build_sends(
        order, owners, generator[0, 0], hamiltonian[0, 0], cross_weights, channels, spread
    )
    got = [sends[0]]
    for shift in range(1, channels):
        pairs = [(c, (c + shift) % channels) for c in range(channels)]
        got.append(lax.ppermute(sends[shift], "chan", pairs))
    got = jnp.stack(got)
    tiles_got = got[:, : 2 * spread * TS].reshape(channels, spread, 2, TS, TS)
    weights_cross = got[(me - owners[me]) % channels, 2 * spread * TS :].reshape(-1)

    mixer = recoupling[recoupling_index[me, 0]]
    column_of = (spread_range[None, :] * channels + source[:, None]).reshape(-1)
    mixer_in = mixer[:, column_of]
    cross = tiles_got.reshape(tile_count, 2, TS, TS)
    generator_mixed = jnp.einsum("ji,ixy->jxy", mixer_in, cross[:, 0], precision=highest)
    hamilton_mixed = jnp.einsum("ji,ixy->jxy", mixer_in, cross[:, 1], precision=highest)
    product = bracket(
        from_tiles(generator_mixed, TS), from_tiles(hamilton_mixed, TS), weights_cross
    )
    mixer_out = mixer[:, (spread_range[None, :] * channels + dest[:, None]).reshape(-1)]
    back = jnp.einsum("ji,jxy->ixy", mixer_out, to_tiles(product, TS), precision=highest)
    back = back.reshape(channels, spread, TS, TS)
    home = [back[0]]
    for shift in range(1, channels):
        pairs = [(c, (c + shift) % channels) for c in range(channels)]
        home.append(lax.ppermute(back[shift], "chan", pairs))
    place = order[(source[:, None] * spread + spread_range[None, :]).reshape(-1)]

    direct = bracket(generator[0, 0], hamiltonian[0, 0], pair_weights[0, 0])
    return finish(0.5 * (direct + direct.T), home, place)[None, None]


def solution(mesh):
    placed = (
        P(("groups", "chan"), ("tile", "rep"), None, None),
        P(("groups", "chan"), ("tile", "rep"), None, None),
        P(("groups", "chan"), ("tile", "rep"), None),
        P(("groups", "chan"), ("tile", "rep"), None, None),
        P(),
        P("groups", ("tile", "rep")),
        P(("groups", "chan"), ("tile", "rep"), None),
        P("groups", ("tile", "rep")),
    )
    return jax.shard_map(
        body,
        mesh=mesh,
        in_specs=placed,
        out_specs=P(("groups", "chan"), ("tile", "rep"), None, None),
        check_vma=False,
    )
```

```python
import math

import jax
import jax.numpy as jnp
from jax import lax
from jax.sharding import PartitionSpec as P
from jax.experimental import pallas as pl
from jax.experimental.pallas import tpu as pltpu

TS = 128


highest = lax.Precision.HIGH


def to_tiles(matrix, tile_size):
    leading = matrix.shape[:-2]
    blocks = matrix.shape[-1] // tile_size
    shaped = matrix.reshape(leading + (blocks, tile_size, blocks, tile_size))
    shaped = jnp.swapaxes(shaped, -3, -2)
    return shaped.reshape(leading + (blocks * blocks, tile_size, tile_size))


def from_tiles(pieces, tile_size):
    leading = pieces.shape[:-3]
    blocks = math.isqrt(pieces.shape[-3])
    shaped = pieces.reshape(leading + (blocks, blocks, tile_size, tile_size))
    shaped = jnp.swapaxes(shaped, -3, -2)
    return shaped.reshape(leading + (blocks * tile_size, blocks * tile_size))


def bracket(left_matrix, right_matrix, weights):
    scaled = weights[..., None, :]
    both_scaled = jnp.concatenate([left_matrix * scaled, right_matrix * scaled], axis=-1)
    both = jnp.concatenate([right_matrix, -left_matrix], axis=-2)
    return jnp.matmul(both_scaled, both, precision=highest)


def build_sends(order, owners, generator, hamiltonian, cross_weights, channels, spread):
    blocks = generator.shape[-1] // TS
    capacity, length = cross_weights.shape[-2:]
    rows = 2 * spread * TS + length // TS

    def kernel(order_ref, owner_ref, gen_ref, ham_ref, weight_ref, *outs):
        me = lax.axis_index("chan")
        for s in range(channels):
            g = (me + s) % channels
            for r in range(spread):
                tile = order_ref[g * spread + r]
                top = pl.multiple_of((tile // blocks) * TS, TS)
                left = pl.multiple_of((tile % blocks) * TS, TS)
                for m, src in enumerate((gen_ref, ham_ref)):
                    outs[s][(2 * r + m) * TS:(2 * r + m + 1) * TS, :] = src[
                        pl.ds(top, TS), pl.ds(left, TS)
                    ]
            mine = owner_ref[g]
            slot = 0
            for other in range(channels - 1):
                slot = slot + jnp.where((other < g) & (owner_ref[other] == mine), 1, 0)
            slot = jnp.minimum(slot, capacity - 1)
            for c in range(length // TS):
                row = 2 * spread * TS + c
                rows_here = weight_ref[0, 0, :, c * TS:(c + 1) * TS]
                value = rows_here[0:1]
                for q in range(1, capacity):
                    value = jnp.where(slot == q, rows_here[q:q + 1], value)
                outs[s][row:row + 1, :] = value

    whole = pl.BlockSpec(memory_space=pltpu.VMEM)
    return pl.pallas_call(
        kernel,
        grid_spec=pltpu.PrefetchScalarGridSpec(
            num_scalar_prefetch=2,
            grid=(1,),
            in_specs=[whole] * 3,
            out_specs=[whole] * channels,
        ),
        out_shape=[jax.ShapeDtypeStruct((rows, TS), jnp.float32)] * channels,
    )(order, owners, generator, hamiltonian, cross_weights)


def finish(direct, home, place):
    size = direct.shape[-1]
    blocks = size // TS
    spread = home[0].shape[0]

    def kernel(place_ref, direct_ref, *rest):
        pieces, out_ref = rest[:-1], rest[-1]
        out_ref[...] = direct_ref[...]
        for s, piece in enumerate(pieces):
            for r in range(spread):
                tile = place_ref[s * spread + r]
                top = pl.multiple_of((tile // blocks) * TS, TS)
                left = pl.multiple_of((tile % blocks) * TS, TS)
                value = 0.5 * piece[r]
                out_ref[pl.ds(top, TS), pl.ds(left, TS)] += value
                out_ref[pl.ds(left, TS), pl.ds(top, TS)] += value.T

    whole = pl.BlockSpec(memory_space=pltpu.VMEM)
    return pl.pallas_call(
        kernel,
        grid_spec=pltpu.PrefetchScalarGridSpec(
            num_scalar_prefetch=1,
            grid=(1,),
            in_specs=[whole] * (1 + len(home)),
            out_specs=whole,
        ),
        out_shape=jax.ShapeDtypeStruct((size, size), jnp.float32),
    )(place, direct, *home)


def body(
    generator,
    hamiltonian,
    pair_weights,
    cross_weights,
    recoupling,
    cross_owner,
    tile_order,
    recoupling_index,
):
    channels = cross_owner.shape[0]
    tile_count = tile_order.shape[-1]
    spread = tile_count // channels
    capacity = cross_weights.shape[2]
    size = generator.shape[-1]
    me = lax.axis_index("chan")
    chan_range = jnp.arange(channels, dtype=jnp.int32)
    spread_range = jnp.arange(spread, dtype=jnp.int32)

    order = tile_order[0, 0]
    owners = cross_owner[:, 0]

    dest = (me + chan_range) % channels
    source = (me - chan_range) % channels
    sends = build_sends(
        order, owners, generator[0, 0], hamiltonian[0, 0], cross_weights, channels, spread
    )
    got = [sends[0]]
    for shift in range(1, channels):
        pairs = [(c, (c + shift) % channels) for c in range(channels)]
        got.append(lax.ppermute(sends[shift], "chan", pairs))
    got = jnp.stack(got)
    tiles_got = got[:, : 2 * spread * TS].reshape(channels, spread, 2, TS, TS)
    weights_cross = got[(me - owners[me]) % channels, 2 * spread * TS :].reshape(-1)

    mixer = recoupling[recoupling_index[me, 0]]
    column_of = (spread_range[None, :] * channels + source[:, None]).reshape(-1)
    mixer_in = mixer[:, column_of]
    cross = tiles_got.reshape(tile_count, 2, TS, TS)
    generator_mixed = jnp.einsum("ji,ixy->jxy", mixer_in, cross[:, 0], precision=highest)
    hamilton_mixed = jnp.einsum("ji,ixy->jxy", mixer_in, cross[:, 1], precision=highest)
    product = bracket(
        from_tiles(generator_mixed, TS), from_tiles(hamilton_mixed, TS), weights_cross
    )
    mixer_out = mixer[:, (spread_range[None, :] * channels + dest[:, None]).reshape(-1)]
    back = jnp.einsum("ji,jxy->ixy", mixer_out, to_tiles(product, TS), precision=highest)
    back = back.reshape(channels, spread, TS, TS)
    home = [back[0]]
    for shift in range(1, channels):
        pairs = [(c, (c + shift) % channels) for c in range(channels)]
        home.append(lax.ppermute(back[shift], "chan", pairs))
    place = order[(source[:, None] * spread + spread_range[None, :]).reshape(-1)]

    direct = bracket(generator[0, 0], hamiltonian[0, 0], pair_weights[0, 0])
    return finish(0.5 * (direct + direct.T), home, place)[None, None]


def solution(mesh):
    placed = (
        P(("groups", "chan"), ("tile", "rep"), None, None),
        P(("groups", "chan"), ("tile", "rep"), None, None),
        P(("groups", "chan"), ("tile", "rep"), None),
        P(("groups", "chan"), ("tile", "rep"), None, None),
        P(),
        P("groups", ("tile", "rep")),
        P(("groups", "chan"), ("tile", "rep"), None),
        P("groups", ("tile", "rep")),
    )
    return jax.shard_map(
        body,
        mesh=mesh,
        in_specs=placed,
        out_specs=P(("groups", "chan"), ("tile", "rep"), None, None),
        check_vma=False,
    )
```

```python
import math

import jax
import jax.numpy as jnp
from jax import lax
from jax.sharding import PartitionSpec as P
from jax.experimental import pallas as pl
from jax.experimental.pallas import tpu as pltpu

TS = 128


highest = lax.Precision.HIGH


def to_tiles(matrix, tile_size):
    leading = matrix.shape[:-2]
    blocks = matrix.shape[-1] // tile_size
    shaped = matrix.reshape(leading + (blocks, tile_size, blocks, tile_size))
    shaped = jnp.swapaxes(shaped, -3, -2)
    return shaped.reshape(leading + (blocks * blocks, tile_size, tile_size))


def from_tiles(pieces, tile_size):
    leading = pieces.shape[:-3]
    blocks = math.isqrt(pieces.shape[-3])
    shaped = pieces.reshape(leading + (blocks, blocks, tile_size, tile_size))
    shaped = jnp.swapaxes(shaped, -3, -2)
    return shaped.reshape(leading + (blocks * tile_size, blocks * tile_size))


def bracket(left_matrix, right_matrix, weights):
    scaled = weights[..., None, :]
    left_term = jnp.matmul(left_matrix * scaled, right_matrix, precision=highest)
    right_term = jnp.matmul(right_matrix * scaled, left_matrix, precision=highest)
    return left_term - right_term


def build_sends(order, owners, generator, hamiltonian, cross_weights, channels, spread):
    blocks = generator.shape[-1] // TS
    capacity, length = cross_weights.shape[-2:]
    rows = 2 * spread * TS + length // TS

    def kernel(order_ref, owner_ref, gen_ref, ham_ref, weight_ref, *outs):
        me = lax.axis_index("chan")
        for s in range(channels):
            g = (me + s) % channels
            for r in range(spread):
                tile = order_ref[g * spread + r]
                top = pl.multiple_of((tile // blocks) * TS, TS)
                for b in range(blocks):

                    @pl.when(tile % blocks == b)
                    def _(s=s, r=r, b=b, top=top):
                        for m, src in enumerate((gen_ref, ham_ref)):
                            outs[s][(2 * r + m) * TS:(2 * r + m + 1) * TS, :] = src[
                                pl.ds(top, TS), b * TS:(b + 1) * TS
                            ]
            mine = owner_ref[g]
            slot = 0
            for other in range(channels - 1):
                slot = slot + jnp.where((other < g) & (owner_ref[other] == mine), 1, 0)
            slot = jnp.minimum(slot, capacity - 1)
            for c in range(length // TS):
                row = 2 * spread * TS + c
                rows_here = weight_ref[0, 0, :, c * TS:(c + 1) * TS]
                value = rows_here[0:1]
                for q in range(1, capacity):
                    value = jnp.where(slot == q, rows_here[q:q + 1], value)
                outs[s][row:row + 1, :] = value

    whole = pl.BlockSpec(memory_space=pltpu.VMEM)
    return pl.pallas_call(
        kernel,
        grid_spec=pltpu.PrefetchScalarGridSpec(
            num_scalar_prefetch=2,
            grid=(1,),
            in_specs=[whole] * 3,
            out_specs=[whole] * channels,
        ),
        out_shape=[jax.ShapeDtypeStruct((rows, TS), jnp.float32)] * channels,
    )(order, owners, generator, hamiltonian, cross_weights)


def finish(direct, home, place):
    size = direct.shape[-1]
    blocks = size // TS
    spread = home[0].shape[0]

    def kernel(place_ref, direct_ref, *rest):
        pieces, out_ref = rest[:-1], rest[-1]
        out_ref[...] = direct_ref[...]
        for s, piece in enumerate(pieces):
            for r in range(spread):
                tile = place_ref[s * spread + r]
                row, col = tile // blocks, tile % blocks
                top = pl.multiple_of(row * TS, TS)
                left = pl.multiple_of(col * TS, TS)
                for b in range(blocks):

                    @pl.when(col == b)
                    def _(piece=piece, r=r, b=b, top=top):
                        out_ref[pl.ds(top, TS), b * TS:(b + 1) * TS] += 0.5 * piece[r]

                    @pl.when(row == b)
                    def _(piece=piece, r=r, b=b, left=left):
                        out_ref[pl.ds(left, TS), b * TS:(b + 1) * TS] += 0.5 * piece[r].T

    whole = pl.BlockSpec(memory_space=pltpu.VMEM)
    return pl.pallas_call(
        kernel,
        grid_spec=pltpu.PrefetchScalarGridSpec(
            num_scalar_prefetch=1,
            grid=(1,),
            in_specs=[whole] * (1 + len(home)),
            out_specs=whole,
        ),
        out_shape=jax.ShapeDtypeStruct((size, size), jnp.float32),
    )(place, direct, *home)


def body(
    generator,
    hamiltonian,
    pair_weights,
    cross_weights,
    recoupling,
    cross_owner,
    tile_order,
    recoupling_index,
):
    channels = cross_owner.shape[0]
    tile_count = tile_order.shape[-1]
    spread = tile_count // channels
    capacity = cross_weights.shape[2]
    size = generator.shape[-1]
    me = lax.axis_index("chan")
    chan_range = jnp.arange(channels, dtype=jnp.int32)
    spread_range = jnp.arange(spread, dtype=jnp.int32)

    order = tile_order[0, 0]
    owners = cross_owner[:, 0]

    dest = (me + chan_range) % channels
    source = (me - chan_range) % channels
    sends = build_sends(
        order, owners, generator[0, 0], hamiltonian[0, 0], cross_weights, channels, spread
    )
    got = [sends[0]]
    for shift in range(1, channels):
        pairs = [(c, (c + shift) % channels) for c in range(channels)]
        got.append(lax.ppermute(sends[shift], "chan", pairs))
    got = jnp.stack(got)
    tiles_got = got[:, : 2 * spread * TS].reshape(channels, spread, 2, TS, TS)
    weights_cross = got[(me - owners[me]) % channels, 2 * spread * TS :].reshape(-1)

    mixer = recoupling[recoupling_index[me, 0]]
    column_of = (spread_range[None, :] * channels + source[:, None]).reshape(-1)
    mixer_in = mixer[:, column_of]
    cross = tiles_got.reshape(tile_count, 2, TS, TS)
    generator_mixed = jnp.einsum("ji,ixy->jxy", mixer_in, cross[:, 0], precision=highest)
    hamilton_mixed = jnp.einsum("ji,ixy->jxy", mixer_in, cross[:, 1], precision=highest)
    product = bracket(
        from_tiles(generator_mixed, TS), from_tiles(hamilton_mixed, TS), weights_cross
    )
    mixer_out = mixer[:, (spread_range[None, :] * channels + dest[:, None]).reshape(-1)]
    back = jnp.einsum("ji,jxy->ixy", mixer_out, to_tiles(product, TS), precision=highest)
    back = back.reshape(channels, spread, TS, TS)
    home = [back[0]]
    for shift in range(1, channels):
        pairs = [(c, (c + shift) % channels) for c in range(channels)]
        home.append(lax.ppermute(back[shift], "chan", pairs))
    place = order[(source[:, None] * spread + spread_range[None, :]).reshape(-1)]

    direct = bracket(generator[0, 0], hamiltonian[0, 0], pair_weights[0, 0])
    return finish(0.5 * (direct + direct.T), home, place)[None, None]


def solution(mesh):
    placed = (
        P(("groups", "chan"), ("tile", "rep"), None, None),
        P(("groups", "chan"), ("tile", "rep"), None, None),
        P(("groups", "chan"), ("tile", "rep"), None),
        P(("groups", "chan"), ("tile", "rep"), None, None),
        P(),
        P("groups", ("tile", "rep")),
        P(("groups", "chan"), ("tile", "rep"), None),
        P("groups", ("tile", "rep")),
    )
    return jax.shard_map(
        body,
        mesh=mesh,
        in_specs=placed,
        out_specs=P(("groups", "chan"), ("tile", "rep"), None, None),
        check_vma=False,
    )
```

```python
import math

import jax
import jax.numpy as jnp
from jax import lax
from jax.sharding import PartitionSpec as P
from jax.experimental import pallas as pl
from jax.experimental.pallas import tpu as pltpu

TS = 128


highest = lax.Precision.HIGH


def to_tiles(matrix, tile_size):
    leading = matrix.shape[:-2]
    blocks = matrix.shape[-1] // tile_size
    shaped = matrix.reshape(leading + (blocks, tile_size, blocks, tile_size))
    shaped = jnp.swapaxes(shaped, -3, -2)
    return shaped.reshape(leading + (blocks * blocks, tile_size, tile_size))


def from_tiles(pieces, tile_size):
    leading = pieces.shape[:-3]
    blocks = math.isqrt(pieces.shape[-3])
    shaped = pieces.reshape(leading + (blocks, blocks, tile_size, tile_size))
    shaped = jnp.swapaxes(shaped, -3, -2)
    return shaped.reshape(leading + (blocks * tile_size, blocks * tile_size))


def bracket(left_matrix, right_matrix, weights):
    scaled = weights[..., None, :]
    left_term = jnp.matmul(left_matrix * scaled, right_matrix, precision=highest)
    right_term = jnp.matmul(right_matrix * scaled, left_matrix, precision=highest)
    return left_term - right_term


def build_sends(order, owners, generator, hamiltonian, cross_weights, channels, spread):
    blocks = generator.shape[-1] // TS
    capacity, length = cross_weights.shape[-2:]
    rows = 2 * spread * TS + length // TS

    def kernel(order_ref, owner_ref, gen_ref, ham_ref, weight_ref, *outs):
        me = lax.axis_index("chan")
        for s in range(channels):
            g = (me + s) % channels
            for r in range(spread):
                tile = order_ref[g * spread + r]
                top = pl.multiple_of((tile // blocks) * TS, TS)
                left = pl.multiple_of((tile % blocks) * TS, TS)
                for m, src in enumerate((gen_ref, ham_ref)):
                    outs[s][(2 * r + m) * TS:(2 * r + m + 1) * TS, :] = src[
                        pl.ds(top, TS), pl.ds(left, TS)
                    ]
            mine = owner_ref[g]
            slot = 0
            for other in range(channels - 1):
                slot = slot + jnp.where((other < g) & (owner_ref[other] == mine), 1, 0)
            slot = jnp.minimum(slot, capacity - 1)
            for c in range(length // TS):
                row = 2 * spread * TS + c
                rows_here = weight_ref[0, 0, :, c * TS:(c + 1) * TS]
                value = rows_here[0:1]
                for q in range(1, capacity):
                    value = jnp.where(slot == q, rows_here[q:q + 1], value)
                outs[s][row:row + 1, :] = value

    whole = pl.BlockSpec(memory_space=pltpu.VMEM)
    return pl.pallas_call(
        kernel,
        grid_spec=pltpu.PrefetchScalarGridSpec(
            num_scalar_prefetch=2,
            grid=(1,),
            in_specs=[whole] * 3,
            out_specs=[whole] * channels,
        ),
        out_shape=[jax.ShapeDtypeStruct((rows, TS), jnp.float32)] * channels,
    )(order, owners, generator, hamiltonian, cross_weights)


def finish(direct, home, place):
    size = direct.shape[-1]
    blocks = size // TS
    channels, spread = home.shape[:2]

    def kernel(place_ref, direct_ref, home_ref, out_ref):
        pieces = [home_ref.at[s] for s in range(channels)]
        out_ref[...] = direct_ref[...]
        for s, piece in enumerate(pieces):
            for r in range(spread):
                tile = place_ref[s * spread + r]
                top = pl.multiple_of((tile // blocks) * TS, TS)
                left = pl.multiple_of((tile % blocks) * TS, TS)
                value = 0.5 * piece[r]
                out_ref[pl.ds(top, TS), pl.ds(left, TS)] += value
                out_ref[pl.ds(left, TS), pl.ds(top, TS)] += value.T

    whole = pl.BlockSpec(memory_space=pltpu.VMEM)
    return pl.pallas_call(
        kernel,
        grid_spec=pltpu.PrefetchScalarGridSpec(
            num_scalar_prefetch=1,
            grid=(1,),
            in_specs=[whole] * 2,
            out_specs=whole,
        ),
        out_shape=jax.ShapeDtypeStruct((size, size), jnp.float32),
    )(place, direct, home)


def body(
    generator,
    hamiltonian,
    pair_weights,
    cross_weights,
    recoupling,
    cross_owner,
    tile_order,
    recoupling_index,
):
    channels = cross_owner.shape[0]
    tile_count = tile_order.shape[-1]
    spread = tile_count // channels
    capacity = cross_weights.shape[2]
    size = generator.shape[-1]
    me = lax.axis_index("chan")
    chan_range = jnp.arange(channels, dtype=jnp.int32)
    spread_range = jnp.arange(spread, dtype=jnp.int32)

    order = tile_order[0, 0]
    owners = cross_owner[:, 0]

    dest = (me + chan_range) % channels
    source = (me - chan_range) % channels
    sends = build_sends(
        order, owners, generator[0, 0], hamiltonian[0, 0], cross_weights, channels, spread
    )
    got = [sends[0]]
    for shift in range(1, channels):
        pairs = [(c, (c + shift) % channels) for c in range(channels)]
        got.append(lax.ppermute(sends[shift], "chan", pairs))
    got = jnp.stack(got)
    tiles_got = got[:, : 2 * spread * TS].reshape(channels, spread, 2, TS, TS)
    weights_cross = got[(me - owners[me]) % channels, 2 * spread * TS :].reshape(-1)

    mixer = recoupling[recoupling_index[me, 0]]
    column_of = (spread_range[None, :] * channels + source[:, None]).reshape(-1)
    mixer_in = mixer[:, column_of]
    cross = tiles_got.reshape(tile_count, 2, TS, TS)
    generator_mixed = jnp.einsum("ji,ixy->jxy", mixer_in, cross[:, 0], precision=highest)
    hamilton_mixed = jnp.einsum("ji,ixy->jxy", mixer_in, cross[:, 1], precision=highest)
    product = bracket(
        from_tiles(generator_mixed, TS), from_tiles(hamilton_mixed, TS), weights_cross
    )
    back = jnp.einsum("ji,jxy->ixy", mixer, to_tiles(product, TS), precision=highest)
    back = jnp.swapaxes(back.reshape(spread, channels, TS, TS), 0, 1)
    home = lax.all_to_all(back, "chan", 0, 0, tiled=True)

    direct = bracket(generator[0, 0], hamiltonian[0, 0], pair_weights[0, 0])
    return finish(0.5 * (direct + direct.T), home, order)[None, None]


def solution(mesh):
    placed = (
        P(("groups", "chan"), ("tile", "rep"), None, None),
        P(("groups", "chan"), ("tile", "rep"), None, None),
        P(("groups", "chan"), ("tile", "rep"), None),
        P(("groups", "chan"), ("tile", "rep"), None, None),
        P(),
        P("groups", ("tile", "rep")),
        P(("groups", "chan"), ("tile", "rep"), None),
        P("groups", ("tile", "rep")),
    )
    return jax.shard_map(
        body,
        mesh=mesh,
        in_specs=placed,
        out_specs=P(("groups", "chan"), ("tile", "rep"), None, None),
        check_vma=False,
    )
```

```python
import math

import jax
import jax.numpy as jnp
from jax import lax
from jax.sharding import PartitionSpec as P
from jax.experimental import pallas as pl
from jax.experimental.pallas import tpu as pltpu

TS = 128


highest = lax.Precision.HIGH


def to_tiles(matrix, tile_size):
    leading = matrix.shape[:-2]
    blocks = matrix.shape[-1] // tile_size
    shaped = matrix.reshape(leading + (blocks, tile_size, blocks, tile_size))
    shaped = jnp.swapaxes(shaped, -3, -2)
    return shaped.reshape(leading + (blocks * blocks, tile_size, tile_size))


def from_tiles(pieces, tile_size):
    leading = pieces.shape[:-3]
    blocks = math.isqrt(pieces.shape[-3])
    shaped = pieces.reshape(leading + (blocks, blocks, tile_size, tile_size))
    shaped = jnp.swapaxes(shaped, -3, -2)
    return shaped.reshape(leading + (blocks * tile_size, blocks * tile_size))


def bracket(left_matrix, right_matrix, weights):
    scaled = weights[..., None, :]
    left_term = jnp.matmul(left_matrix * scaled, right_matrix, precision=highest)
    right_term = jnp.matmul(right_matrix * scaled, left_matrix, precision=highest)
    return left_term - right_term


def build_sends(order, owners, generator, hamiltonian, cross_weights, channels, spread):
    blocks = generator.shape[-1] // TS
    capacity, length = cross_weights.shape[-2:]
    rows = 2 * spread * TS + length // TS

    def kernel(order_ref, owner_ref, gen_ref, ham_ref, weight_ref, *outs):
        me = lax.axis_index("chan")
        for s in range(channels):
            g = (me + s) % channels
            for r in range(spread):
                tile = order_ref[g * spread + r]
                top = pl.multiple_of((tile // blocks) * TS, TS)
                left = pl.multiple_of((tile % blocks) * TS, TS)
                for m, src in enumerate((gen_ref, ham_ref)):
                    outs[s][(2 * r + m) * TS:(2 * r + m + 1) * TS, :] = src[
                        pl.ds(top, TS), pl.ds(left, TS)
                    ]
            mine = owner_ref[g]
            slot = 0
            for other in range(channels - 1):
                slot = slot + jnp.where((other < g) & (owner_ref[other] == mine), 1, 0)
            slot = jnp.minimum(slot, capacity - 1)
            for c in range(length // TS):
                row = 2 * spread * TS + c
                rows_here = weight_ref[0, 0, :, c * TS:(c + 1) * TS]
                value = rows_here[0:1]
                for q in range(1, capacity):
                    value = jnp.where(slot == q, rows_here[q:q + 1], value)
                outs[s][row:row + 1, :] = value

    whole = pl.BlockSpec(memory_space=pltpu.VMEM)
    return pl.pallas_call(
        kernel,
        grid_spec=pltpu.PrefetchScalarGridSpec(
            num_scalar_prefetch=2,
            grid=(1,),
            in_specs=[whole] * 3,
            out_specs=[whole] * channels,
        ),
        out_shape=[jax.ShapeDtypeStruct((rows, TS), jnp.float32)] * channels,
    )(order, owners, generator, hamiltonian, cross_weights)


def finish(direct, home, place):
    size = direct.shape[-1]
    blocks = size // TS
    spread = home[0].shape[0]

    def kernel(place_ref, direct_ref, *rest):
        pieces, out_ref = rest[:-1], rest[-1]
        out_ref[...] = direct_ref[...]
        for s, piece in enumerate(pieces):
            for r in range(spread):
                tile = place_ref[s * spread + r]
                top = pl.multiple_of((tile // blocks) * TS, TS)
                left = pl.multiple_of((tile % blocks) * TS, TS)
                value = 0.5 * piece[r]
                out_ref[pl.ds(top, TS), pl.ds(left, TS)] += value
                out_ref[pl.ds(left, TS), pl.ds(top, TS)] += value.T

    whole = pl.BlockSpec(memory_space=pltpu.VMEM)
    return pl.pallas_call(
        kernel,
        grid_spec=pltpu.PrefetchScalarGridSpec(
            num_scalar_prefetch=1,
            grid=(1,),
            in_specs=[whole] * (1 + len(home)),
            out_specs=whole,
        ),
        out_shape=jax.ShapeDtypeStruct((size, size), jnp.float32),
    )(place, direct, *home)


def body(
    generator,
    hamiltonian,
    pair_weights,
    cross_weights,
    recoupling,
    cross_owner,
    tile_order,
    recoupling_index,
):
    channels = cross_owner.shape[0]
    tile_count = tile_order.shape[-1]
    spread = tile_count // channels
    capacity = cross_weights.shape[2]
    size = generator.shape[-1]
    me = lax.axis_index("chan")
    chan_range = jnp.arange(channels, dtype=jnp.int32)
    spread_range = jnp.arange(spread, dtype=jnp.int32)

    order = tile_order[0, 0]
    owners = cross_owner[:, 0]

    dest = (me + chan_range) % channels
    source = (me - chan_range) % channels
    sends = build_sends(
        order, owners, generator[0, 0], hamiltonian[0, 0], cross_weights, channels, spread
    )
    got = [sends[0]]
    for shift in range(1, channels):
        pairs = [(c, (c + shift) % channels) for c in range(channels)]
        got.append(lax.ppermute(sends[shift], "chan", pairs))
    got = jnp.stack(got)
    tiles_got = got[:, : 2 * spread * TS].reshape(channels, spread, 2, TS, TS)
    weights_cross = got[(me - owners[me]) % channels, 2 * spread * TS :].reshape(-1)

    mixer = recoupling[recoupling_index[me, 0]]
    column_of = (spread_range[None, :] * channels + source[:, None]).reshape(-1)
    mixer_in = mixer[:, column_of]
    cross = tiles_got.reshape(tile_count, 2, TS, TS)
    mixed = from_tiles(jnp.einsum("ji,imxy->mjxy", mixer_in, cross, precision=highest), TS)
    scaled = mixed * weights_cross[None, None, :]
    terms = jnp.einsum("kij,kjl->kil", scaled, mixed[::-1], precision=highest)
    product = terms[0] - terms[1]
    mixer_out = mixer[:, (spread_range[None, :] * channels + dest[:, None]).reshape(-1)]
    back = jnp.einsum("ji,jxy->ixy", mixer_out, to_tiles(product, TS), precision=highest)
    back = back.reshape(channels, spread, TS, TS)
    home = [back[0]]
    for shift in range(1, channels):
        pairs = [(c, (c + shift) % channels) for c in range(channels)]
        home.append(lax.ppermute(back[shift], "chan", pairs))
    place = order[(source[:, None] * spread + spread_range[None, :]).reshape(-1)]

    direct = bracket(generator[0, 0], hamiltonian[0, 0], pair_weights[0, 0])
    return finish(0.5 * (direct + direct.T), home, place)[None, None]


def solution(mesh):
    placed = (
        P(("groups", "chan"), ("tile", "rep"), None, None),
        P(("groups", "chan"), ("tile", "rep"), None, None),
        P(("groups", "chan"), ("tile", "rep"), None),
        P(("groups", "chan"), ("tile", "rep"), None, None),
        P(),
        P("groups", ("tile", "rep")),
        P(("groups", "chan"), ("tile", "rep"), None),
        P("groups", ("tile", "rep")),
    )
    return jax.shard_map(
        body,
        mesh=mesh,
        in_specs=placed,
        out_specs=P(("groups", "chan"), ("tile", "rep"), None, None),
        check_vma=False,
    )
```

```python
import math

import jax
import jax.numpy as jnp
from jax import lax
from jax.sharding import PartitionSpec as P
from jax.experimental import pallas as pl
from jax.experimental.pallas import tpu as pltpu

TS = 128


highest = lax.Precision.HIGH


def to_tiles(matrix, tile_size):
    leading = matrix.shape[:-2]
    blocks = matrix.shape[-1] // tile_size
    shaped = matrix.reshape(leading + (blocks, tile_size, blocks, tile_size))
    shaped = jnp.swapaxes(shaped, -3, -2)
    return shaped.reshape(leading + (blocks * blocks, tile_size, tile_size))


def from_tiles(pieces, tile_size):
    leading = pieces.shape[:-3]
    blocks = math.isqrt(pieces.shape[-3])
    shaped = pieces.reshape(leading + (blocks, blocks, tile_size, tile_size))
    shaped = jnp.swapaxes(shaped, -3, -2)
    return shaped.reshape(leading + (blocks * tile_size, blocks * tile_size))


def bracket(left_matrix, right_matrix, weights):
    scaled = weights[..., None, :]
    left_term = jnp.matmul(left_matrix * scaled, right_matrix, precision=highest)
    right_term = jnp.matmul(right_matrix * scaled, left_matrix, precision=highest)
    return left_term - right_term


def build_sends(order, owners, generator, hamiltonian, cross_weights, channels, spread):
    blocks = generator.shape[-1] // TS
    capacity, length = cross_weights.shape[-2:]
    rows = 2 * spread * TS + length // TS

    def kernel(order_ref, owner_ref, gen_ref, ham_ref, weight_ref, *outs):
        me = lax.axis_index("chan")
        for s in range(channels):
            g = (me + s) % channels
            for r in range(spread):
                tile = order_ref[g * spread + r]
                top = pl.multiple_of((tile // blocks) * TS, TS)
                left = pl.multiple_of((tile % blocks) * TS, TS)
                for m, src in enumerate((gen_ref, ham_ref)):
                    outs[s][(2 * r + m) * TS:(2 * r + m + 1) * TS, :] = src[
                        pl.ds(top, TS), pl.ds(left, TS)
                    ]
            mine = owner_ref[g]
            slot = 0
            for other in range(channels - 1):
                slot = slot + jnp.where((other < g) & (owner_ref[other] == mine), 1, 0)
            slot = jnp.minimum(slot, capacity - 1)
            for c in range(length // TS):
                row = 2 * spread * TS + c
                rows_here = weight_ref[0, 0, :, c * TS:(c + 1) * TS]
                value = rows_here[0:1]
                for q in range(1, capacity):
                    value = jnp.where(slot == q, rows_here[q:q + 1], value)
                outs[s][row:row + 1, :] = value

    whole = pl.BlockSpec(memory_space=pltpu.VMEM)
    return pl.pallas_call(
        kernel,
        grid_spec=pltpu.PrefetchScalarGridSpec(
            num_scalar_prefetch=2,
            grid=(1,),
            in_specs=[whole] * 3,
            out_specs=[whole] * channels,
        ),
        out_shape=[jax.ShapeDtypeStruct((rows, TS), jnp.float32)] * channels,
    )(order, owners, generator, hamiltonian, cross_weights)


def finish(direct, home, place):
    size = direct.shape[-1]
    blocks = size // TS
    spread = home[0].shape[0]

    def kernel(place_ref, direct_ref, *rest):
        pieces, out_ref = rest[:-1], rest[-1]
        out_ref[...] = direct_ref[...]
        for s, piece in enumerate(pieces):
            for r in range(spread):
                tile = place_ref[s * spread + r]
                top = pl.multiple_of((tile // blocks) * TS, TS)
                left = pl.multiple_of((tile % blocks) * TS, TS)
                value = 0.5 * piece[r]
                out_ref[pl.ds(top, TS), pl.ds(left, TS)] += value
                out_ref[pl.ds(left, TS), pl.ds(top, TS)] += value.T

    whole = pl.BlockSpec(memory_space=pltpu.VMEM)
    return pl.pallas_call(
        kernel,
        grid_spec=pltpu.PrefetchScalarGridSpec(
            num_scalar_prefetch=1,
            grid=(1,),
            in_specs=[whole] * (1 + len(home)),
            out_specs=whole,
        ),
        out_shape=jax.ShapeDtypeStruct((size, size), jnp.float32),
    )(place, direct, *home)


def body(
    generator,
    hamiltonian,
    pair_weights,
    cross_weights,
    recoupling,
    cross_owner,
    tile_order,
    recoupling_index,
):
    channels = cross_owner.shape[0]
    tile_count = tile_order.shape[-1]
    spread = tile_count // channels
    capacity = cross_weights.shape[2]
    size = generator.shape[-1]
    me = lax.axis_index("chan")
    chan_range = jnp.arange(channels, dtype=jnp.int32)
    spread_range = jnp.arange(spread, dtype=jnp.int32)

    order = tile_order[0, 0]
    owners = cross_owner[:, 0]

    dest = (me + chan_range) % channels
    source = (me - chan_range) % channels
    sends = build_sends(
        order, owners, generator[0, 0], hamiltonian[0, 0], cross_weights, channels, spread
    )
    got = [sends[0]]
    for shift in range(1, channels):
        pairs = [(c, (c + shift) % channels) for c in range(channels)]
        got.append(lax.ppermute(sends[shift], "chan", pairs))
    got = jnp.stack(got)
    tiles_got = got[:, : 2 * spread * TS].reshape(channels, spread, 2, TS, TS)
    weights_cross = got[(me - owners[me]) % channels, 2 * spread * TS :].reshape(-1)

    mixer = recoupling[recoupling_index[me, 0]]
    column_of = (spread_range[None, :] * channels + source[:, None]).reshape(-1)
    mixer_in = mixer[:, column_of]
    cross = tiles_got.reshape(tile_count, 2, TS, TS)
    generator_mixed = jnp.einsum("ji,ixy->jxy", mixer_in, cross[:, 0], precision=highest)
    hamilton_mixed = jnp.einsum("ji,ixy->jxy", mixer_in, cross[:, 1], precision=highest)
    product = bracket(
        from_tiles(generator_mixed, TS), from_tiles(hamilton_mixed, TS), weights_cross
    )
    back = jnp.einsum("ji,jxy->ixy", mixer, to_tiles(product, TS), precision=highest)
    back = jnp.swapaxes(back.reshape(spread, channels, TS, TS), 0, 1)
    home = [lax.dynamic_index_in_dim(back, dest[0], 0, keepdims=False)]
    for shift in range(1, channels):
        pairs = [(c, (c + shift) % channels) for c in range(channels)]
        piece = lax.dynamic_index_in_dim(back, dest[shift], 0, keepdims=False)
        home.append(lax.ppermute(piece, "chan", pairs))
    place = order[(source[:, None] * spread + spread_range[None, :]).reshape(-1)]

    direct = bracket(generator[0, 0], hamiltonian[0, 0], pair_weights[0, 0])
    return finish(0.5 * (direct + direct.T), home, place)[None, None]


def solution(mesh):
    placed = (
        P(("groups", "chan"), ("tile", "rep"), None, None),
        P(("groups", "chan"), ("tile", "rep"), None, None),
        P(("groups", "chan"), ("tile", "rep"), None),
        P(("groups", "chan"), ("tile", "rep"), None, None),
        P(),
        P("groups", ("tile", "rep")),
        P(("groups", "chan"), ("tile", "rep"), None),
        P("groups", ("tile", "rep")),
    )
    return jax.shard_map(
        body,
        mesh=mesh,
        in_specs=placed,
        out_specs=P(("groups", "chan"), ("tile", "rep"), None, None),
        check_vma=False,
    )
```

```python
import math

import jax
import jax.numpy as jnp
from jax import lax
from jax.sharding import PartitionSpec as P
from jax.experimental import pallas as pl
from jax.experimental.pallas import tpu as pltpu

TS = 128


highest = lax.Precision.HIGH


def to_tiles(matrix, tile_size):
    leading = matrix.shape[:-2]
    blocks = matrix.shape[-1] // tile_size
    shaped = matrix.reshape(leading + (blocks, tile_size, blocks, tile_size))
    shaped = jnp.swapaxes(shaped, -3, -2)
    return shaped.reshape(leading + (blocks * blocks, tile_size, tile_size))


def from_tiles(pieces, tile_size):
    leading = pieces.shape[:-3]
    blocks = math.isqrt(pieces.shape[-3])
    shaped = pieces.reshape(leading + (blocks, blocks, tile_size, tile_size))
    shaped = jnp.swapaxes(shaped, -3, -2)
    return shaped.reshape(leading + (blocks * tile_size, blocks * tile_size))


def bracket(left_matrix, right_matrix, weights):
    scaled = weights[..., None, :]
    left_term = jnp.matmul(left_matrix * scaled, right_matrix, precision=highest)
    right_term = jnp.matmul(right_matrix * scaled, left_matrix, precision=highest)
    return left_term - right_term


def build_sends(order, owners, generator, hamiltonian, cross_weights, channels, spread):
    blocks = generator.shape[-1] // TS
    capacity, length = cross_weights.shape[-2:]
    rows = 2 * spread * TS + length // TS

    def kernel(order_ref, owner_ref, gen_ref, ham_ref, weight_ref, *outs):
        outs = (None,) + outs
        me = lax.axis_index("chan")
        for s in range(1, channels):
            g = (me + s) % channels
            for r in range(spread):
                tile = order_ref[g * spread + r]
                top = pl.multiple_of((tile // blocks) * TS, TS)
                left = pl.multiple_of((tile % blocks) * TS, TS)
                for m, src in enumerate((gen_ref, ham_ref)):
                    outs[s][(2 * r + m) * TS:(2 * r + m + 1) * TS, :] = src[
                        pl.ds(top, TS), pl.ds(left, TS)
                    ]
            mine = owner_ref[g]
            slot = 0
            for other in range(channels - 1):
                slot = slot + jnp.where((other < g) & (owner_ref[other] == mine), 1, 0)
            slot = jnp.minimum(slot, capacity - 1)
            for c in range(length // TS):
                row = 2 * spread * TS + c
                rows_here = weight_ref[0, 0, :, c * TS:(c + 1) * TS]
                value = rows_here[0:1]
                for q in range(1, capacity):
                    value = jnp.where(slot == q, rows_here[q:q + 1], value)
                outs[s][row:row + 1, :] = value

    whole = pl.BlockSpec(memory_space=pltpu.VMEM)
    return pl.pallas_call(
        kernel,
        grid_spec=pltpu.PrefetchScalarGridSpec(
            num_scalar_prefetch=2,
            grid=(1,),
            in_specs=[whole] * 3,
            out_specs=[whole] * (channels - 1),
        ),
        out_shape=[jax.ShapeDtypeStruct((rows, TS), jnp.float32)] * (channels - 1),
    )(order, owners, generator, hamiltonian, cross_weights)


def finish(direct, home, place):
    size = direct.shape[-1]
    blocks = size // TS
    spread = home[0].shape[0]

    def kernel(place_ref, direct_ref, *rest):
        pieces, out_ref = rest[:-1], rest[-1]
        out_ref[...] = direct_ref[...]
        for s, piece in enumerate(pieces):
            for r in range(spread):
                tile = place_ref[s * spread + r]
                top = pl.multiple_of((tile // blocks) * TS, TS)
                left = pl.multiple_of((tile % blocks) * TS, TS)
                value = 0.5 * piece[r]
                out_ref[pl.ds(top, TS), pl.ds(left, TS)] += value
                out_ref[pl.ds(left, TS), pl.ds(top, TS)] += value.T

    whole = pl.BlockSpec(memory_space=pltpu.VMEM)
    return pl.pallas_call(
        kernel,
        grid_spec=pltpu.PrefetchScalarGridSpec(
            num_scalar_prefetch=1,
            grid=(1,),
            in_specs=[whole] * (1 + len(home)),
            out_specs=whole,
        ),
        out_shape=jax.ShapeDtypeStruct((size, size), jnp.float32),
    )(place, direct, *home)


def body(
    generator,
    hamiltonian,
    pair_weights,
    cross_weights,
    recoupling,
    cross_owner,
    tile_order,
    recoupling_index,
):
    channels = cross_owner.shape[0]
    tile_count = tile_order.shape[-1]
    spread = tile_count // channels
    capacity = cross_weights.shape[2]
    size = generator.shape[-1]
    me = lax.axis_index("chan")
    chan_range = jnp.arange(channels, dtype=jnp.int32)
    spread_range = jnp.arange(spread, dtype=jnp.int32)

    order = tile_order[0, 0]
    owners = cross_owner[:, 0]

    dest = (me + chan_range) % channels
    source = (me - chan_range) % channels
    sends = build_sends(
        order, owners, generator[0, 0], hamiltonian[0, 0], cross_weights, channels, spread
    )
    got = [None]
    for shift in range(1, channels):
        pairs = [(c, (c + shift) % channels) for c in range(channels)]
        got.append(lax.ppermute(sends[shift - 1], "chan", pairs))
    earlier = chan_range < me
    slot = jnp.minimum(jnp.sum(earlier & (owners == owners[me])), capacity - 1)
    picked = order[me * spread + spread_range]
    local = jnp.stack(
        [to_tiles(generator[0, 0], TS)[picked], to_tiles(hamiltonian[0, 0], TS)[picked]], axis=1
    ).reshape(2 * spread * TS, TS)
    got[0] = jnp.concatenate([local, cross_weights[0, 0][slot].reshape(-1, TS)], axis=0)
    got = jnp.stack(got)
    tiles_got = got[:, : 2 * spread * TS].reshape(channels, spread, 2, TS, TS)
    weights_cross = got[(me - owners[me]) % channels, 2 * spread * TS :].reshape(-1)

    mixer = recoupling[recoupling_index[me, 0]]
    column_of = (spread_range[None, :] * channels + source[:, None]).reshape(-1)
    mixer_in = mixer[:, column_of]
    cross = tiles_got.reshape(tile_count, 2, TS, TS)
    generator_mixed = jnp.einsum("ji,ixy->jxy", mixer_in, cross[:, 0], precision=highest)
    hamilton_mixed = jnp.einsum("ji,ixy->jxy", mixer_in, cross[:, 1], precision=highest)
    product = bracket(
        from_tiles(generator_mixed, TS), from_tiles(hamilton_mixed, TS), weights_cross
    )
    mixer_out = mixer[:, (spread_range[None, :] * channels + dest[:, None]).reshape(-1)]
    back = jnp.einsum("ji,jxy->ixy", mixer_out, to_tiles(product, TS), precision=highest)
    back = back.reshape(channels, spread, TS, TS)
    home = [back[0]]
    for shift in range(1, channels):
        pairs = [(c, (c + shift) % channels) for c in range(channels)]
        home.append(lax.ppermute(back[shift], "chan", pairs))
    place = order[(source[:, None] * spread + spread_range[None, :]).reshape(-1)]

    direct = bracket(generator[0, 0], hamiltonian[0, 0], pair_weights[0, 0])
    return finish(0.5 * (direct + direct.T), home, place)[None, None]


def solution(mesh):
    placed = (
        P(("groups", "chan"), ("tile", "rep"), None, None),
        P(("groups", "chan"), ("tile", "rep"), None, None),
        P(("groups", "chan"), ("tile", "rep"), None),
        P(("groups", "chan"), ("tile", "rep"), None, None),
        P(),
        P("groups", ("tile", "rep")),
        P(("groups", "chan"), ("tile", "rep"), None),
        P("groups", ("tile", "rep")),
    )
    return jax.shard_map(
        body,
        mesh=mesh,
        in_specs=placed,
        out_specs=P(("groups", "chan"), ("tile", "rep"), None, None),
        check_vma=False,
    )
```

```python
import math

import jax
import jax.numpy as jnp
from jax import lax
from jax.sharding import PartitionSpec as P
from jax.experimental import pallas as pl
from jax.experimental.pallas import tpu as pltpu

TS = 128


highest = lax.Precision.HIGH


def to_tiles(matrix, tile_size):
    leading = matrix.shape[:-2]
    blocks = matrix.shape[-1] // tile_size
    shaped = matrix.reshape(leading + (blocks, tile_size, blocks, tile_size))
    shaped = jnp.swapaxes(shaped, -3, -2)
    return shaped.reshape(leading + (blocks * blocks, tile_size, tile_size))


def from_tiles(pieces, tile_size):
    leading = pieces.shape[:-3]
    blocks = math.isqrt(pieces.shape[-3])
    shaped = pieces.reshape(leading + (blocks, blocks, tile_size, tile_size))
    shaped = jnp.swapaxes(shaped, -3, -2)
    return shaped.reshape(leading + (blocks * tile_size, blocks * tile_size))


def bracket(left_matrix, right_matrix, weights):
    scaled = weights[..., None, :]
    left_term = jnp.matmul(left_matrix * scaled, right_matrix, precision=highest)
    right_term = jnp.matmul(right_matrix * scaled, left_matrix, precision=highest)
    return left_term - right_term


def build_sends(order, owners, generator, hamiltonian, cross_weights, channels, spread):
    blocks = generator.shape[-1] // TS
    capacity, length = cross_weights.shape[-2:]
    rows = 2 * spread * TS + length // TS

    def kernel(order_ref, owner_ref, gen_ref, ham_ref, weight_ref, *outs):
        outs = (None,) + outs
        me = lax.axis_index("chan")
        for s in range(1, channels):
            g = (me + s) % channels
            for r in range(spread):
                tile = order_ref[g * spread + r]
                top = pl.multiple_of((tile // blocks) * TS, TS)
                left = pl.multiple_of((tile % blocks) * TS, TS)
                for m, src in enumerate((gen_ref, ham_ref)):
                    outs[s][(2 * r + m) * TS:(2 * r + m + 1) * TS, :] = src[
                        pl.ds(top, TS), pl.ds(left, TS)
                    ]
            mine = owner_ref[g]
            slot = 0
            for other in range(channels - 1):
                slot = slot + jnp.where((other < g) & (owner_ref[other] == mine), 1, 0)
            slot = jnp.minimum(slot, capacity - 1)
            for c in range(length // TS):
                row = 2 * spread * TS + c
                rows_here = weight_ref[0, 0, :, c * TS:(c + 1) * TS]
                value = rows_here[0:1]
                for q in range(1, capacity):
                    value = jnp.where(slot == q, rows_here[q:q + 1], value)
                outs[s][row:row + 1, :] = value

    whole = pl.BlockSpec(memory_space=pltpu.VMEM)
    return pl.pallas_call(
        kernel,
        grid_spec=pltpu.PrefetchScalarGridSpec(
            num_scalar_prefetch=2,
            grid=(1,),
            in_specs=[whole] * 3,
            out_specs=[whole] * (channels - 1),
        ),
        out_shape=[jax.ShapeDtypeStruct((rows, TS), jnp.float32)] * (channels - 1),
    )(order, owners, generator, hamiltonian, cross_weights)


def finish(direct, home, place):
    size = direct.shape[-1]
    blocks = size // TS
    spread = home[0].shape[0]

    def kernel(place_ref, direct_ref, *rest):
        pieces, out_ref = rest[:-1], rest[-1]
        out_ref[...] = direct_ref[...]
        for s, piece in enumerate(pieces):
            for r in range(spread):
                tile = place_ref[s * spread + r]
                top = pl.multiple_of((tile // blocks) * TS, TS)
                left = pl.multiple_of((tile % blocks) * TS, TS)
                value = 0.5 * piece[r]
                out_ref[pl.ds(top, TS), pl.ds(left, TS)] += value
                out_ref[pl.ds(left, TS), pl.ds(top, TS)] += value.T

    whole = pl.BlockSpec(memory_space=pltpu.VMEM)
    return pl.pallas_call(
        kernel,
        grid_spec=pltpu.PrefetchScalarGridSpec(
            num_scalar_prefetch=1,
            grid=(1,),
            in_specs=[whole] * (1 + len(home)),
            out_specs=whole,
        ),
        out_shape=jax.ShapeDtypeStruct((size, size), jnp.float32),
    )(place, direct, *home)


def body(
    generator,
    hamiltonian,
    pair_weights,
    cross_weights,
    recoupling,
    cross_owner,
    tile_order,
    recoupling_index,
):
    channels = cross_owner.shape[0]
    tile_count = tile_order.shape[-1]
    spread = tile_count // channels
    capacity = cross_weights.shape[2]
    size = generator.shape[-1]
    me = lax.axis_index("chan")
    chan_range = jnp.arange(channels, dtype=jnp.int32)
    spread_range = jnp.arange(spread, dtype=jnp.int32)

    order = tile_order[0, 0]
    owners = cross_owner[:, 0]

    dest = (me + chan_range) % channels
    source = (me - chan_range) % channels
    sends = build_sends(
        order, owners, generator[0, 0], hamiltonian[0, 0], cross_weights, channels, spread
    )
    got = [None]
    for shift in range(1, channels):
        pairs = [(c, (c + shift) % channels) for c in range(channels)]
        got.append(lax.ppermute(sends[shift - 1], "chan", pairs))
    earlier = chan_range < me
    slot = jnp.minimum(jnp.sum(earlier & (owners == owners[me])), capacity - 1)
    picked = order[me * spread + spread_range]
    local = jnp.stack(
        [to_tiles(generator[0, 0], TS)[picked], to_tiles(hamiltonian[0, 0], TS)[picked]], axis=1
    ).reshape(2 * spread * TS, TS)
    got[0] = jnp.concatenate([local, cross_weights[0, 0][slot].reshape(-1, TS)], axis=0)
    stacked = jnp.zeros((channels,) + got[0].shape, jnp.float32)
    for shift, piece in enumerate(got):
        stacked = stacked.at[shift].set(piece)
    got = stacked
    tiles_got = got[:, : 2 * spread * TS].reshape(channels, spread, 2, TS, TS)
    weights_cross = got[(me - owners[me]) % channels, 2 * spread * TS :].reshape(-1)

    mixer = recoupling[recoupling_index[me, 0]]
    column_of = (spread_range[None, :] * channels + source[:, None]).reshape(-1)
    mixer_in = mixer[:, column_of]
    cross = tiles_got.reshape(tile_count, 2, TS, TS)
    generator_mixed = jnp.einsum("ji,ixy->jxy", mixer_in, cross[:, 0], precision=highest)
    hamilton_mixed = jnp.einsum("ji,ixy->jxy", mixer_in, cross[:, 1], precision=highest)
    product = bracket(
        from_tiles(generator_mixed, TS), from_tiles(hamilton_mixed, TS), weights_cross
    )
    mixer_out = mixer[:, (spread_range[None, :] * channels + dest[:, None]).reshape(-1)]
    back = jnp.einsum("ji,jxy->ixy", mixer_out, to_tiles(product, TS), precision=highest)
    back = back.reshape(channels, spread, TS, TS)
    home = [back[0]]
    for shift in range(1, channels):
        pairs = [(c, (c + shift) % channels) for c in range(channels)]
        home.append(lax.ppermute(back[shift], "chan", pairs))
    place = order[(source[:, None] * spread + spread_range[None, :]).reshape(-1)]

    direct = bracket(generator[0, 0], hamiltonian[0, 0], pair_weights[0, 0])
    return finish(0.5 * (direct + direct.T), home, place)[None, None]


def solution(mesh):
    placed = (
        P(("groups", "chan"), ("tile", "rep"), None, None),
        P(("groups", "chan"), ("tile", "rep"), None, None),
        P(("groups", "chan"), ("tile", "rep"), None),
        P(("groups", "chan"), ("tile", "rep"), None, None),
        P(),
        P("groups", ("tile", "rep")),
        P(("groups", "chan"), ("tile", "rep"), None),
        P("groups", ("tile", "rep")),
    )
    return jax.shard_map(
        body,
        mesh=mesh,
        in_specs=placed,
        out_specs=P(("groups", "chan"), ("tile", "rep"), None, None),
        check_vma=False,
    )
```

```python
import math

import jax
import jax.numpy as jnp
from jax import lax
from jax.sharding import PartitionSpec as P
from jax.experimental import pallas as pl
from jax.experimental.pallas import tpu as pltpu

TS = 128


highest = lax.Precision.HIGH


def to_tiles(matrix, tile_size):
    leading = matrix.shape[:-2]
    blocks = matrix.shape[-1] // tile_size
    shaped = matrix.reshape(leading + (blocks, tile_size, blocks, tile_size))
    shaped = jnp.swapaxes(shaped, -3, -2)
    return shaped.reshape(leading + (blocks * blocks, tile_size, tile_size))


def from_tiles(pieces, tile_size):
    leading = pieces.shape[:-3]
    blocks = math.isqrt(pieces.shape[-3])
    shaped = pieces.reshape(leading + (blocks, blocks, tile_size, tile_size))
    shaped = jnp.swapaxes(shaped, -3, -2)
    return shaped.reshape(leading + (blocks * tile_size, blocks * tile_size))


def bracket(left_matrix, right_matrix, weights):
    scaled = weights[..., None, :]
    left_term = jnp.matmul(left_matrix * scaled, right_matrix, precision=highest)
    right_term = jnp.matmul(right_matrix * scaled, left_matrix, precision=highest)
    return left_term - right_term


def build_sends(order, owners, generator, hamiltonian, cross_weights, channels, spread):
    blocks = generator.shape[-1] // TS
    capacity, length = cross_weights.shape[-2:]
    rows = 2 * spread * TS + length // TS

    def kernel(order_ref, owner_ref, gen_ref, ham_ref, weight_ref, *outs):
        outs = (None,) + outs
        me = lax.axis_index("chan")
        for s in range(1, channels):
            g = (me + s) % channels
            for r in range(spread):
                tile = order_ref[g * spread + r]
                top = pl.multiple_of((tile // blocks) * TS, TS)
                left = pl.multiple_of((tile % blocks) * TS, TS)
                for m, src in enumerate((gen_ref, ham_ref)):
                    outs[s][(2 * r + m) * TS:(2 * r + m + 1) * TS, :] = src[
                        pl.ds(top, TS), pl.ds(left, TS)
                    ]
            mine = owner_ref[g]
            slot = 0
            for other in range(channels - 1):
                slot = slot + jnp.where((other < g) & (owner_ref[other] == mine), 1, 0)
            slot = jnp.minimum(slot, capacity - 1)
            for c in range(length // TS):
                row = 2 * spread * TS + c
                rows_here = weight_ref[0, 0, :, c * TS:(c + 1) * TS]
                value = rows_here[0:1]
                for q in range(1, capacity):
                    value = jnp.where(slot == q, rows_here[q:q + 1], value)
                outs[s][row:row + 1, :] = value

    whole = pl.BlockSpec(memory_space=pltpu.VMEM)
    return pl.pallas_call(
        kernel,
        grid_spec=pltpu.PrefetchScalarGridSpec(
            num_scalar_prefetch=2,
            grid=(1,),
            in_specs=[whole] * 3,
            out_specs=[whole] * (channels - 1),
        ),
        out_shape=[jax.ShapeDtypeStruct((rows, TS), jnp.float32)] * (channels - 1),
    )(order, owners, generator, hamiltonian, cross_weights)


def finish(direct, home, place):
    size = direct.shape[-1]
    blocks = size // TS
    spread = home[0].shape[0]

    def kernel(place_ref, direct_ref, *rest):
        pieces, out_ref = rest[:-1], rest[-1]
        out_ref[...] = direct_ref[...]
        for s, piece in enumerate(pieces):
            for r in range(spread):
                tile = place_ref[s * spread + r]
                top = pl.multiple_of((tile // blocks) * TS, TS)
                left = pl.multiple_of((tile % blocks) * TS, TS)
                value = 0.5 * piece[r]
                out_ref[pl.ds(top, TS), pl.ds(left, TS)] += value
                out_ref[pl.ds(left, TS), pl.ds(top, TS)] += value.T

    whole = pl.BlockSpec(memory_space=pltpu.VMEM)
    return pl.pallas_call(
        kernel,
        grid_spec=pltpu.PrefetchScalarGridSpec(
            num_scalar_prefetch=1,
            grid=(1,),
            in_specs=[whole] * (1 + len(home)),
            out_specs=whole,
        ),
        out_shape=jax.ShapeDtypeStruct((size, size), jnp.float32),
    )(place, direct, *home)


def body(
    generator,
    hamiltonian,
    pair_weights,
    cross_weights,
    recoupling,
    cross_owner,
    tile_order,
    recoupling_index,
):
    channels = cross_owner.shape[0]
    tile_count = tile_order.shape[-1]
    spread = tile_count // channels
    capacity = cross_weights.shape[2]
    size = generator.shape[-1]
    me = lax.axis_index("chan")
    chan_range = jnp.arange(channels, dtype=jnp.int32)
    spread_range = jnp.arange(spread, dtype=jnp.int32)

    order = tile_order[0, 0]
    owners = cross_owner[:, 0]

    dest = (me + chan_range) % channels
    source = (me - chan_range) % channels
    sends = build_sends(
        order, owners, generator[0, 0], hamiltonian[0, 0], cross_weights, channels, spread
    )
    got = [None]
    for shift in range(1, channels):
        pairs = [(c, (c + shift) % channels) for c in range(channels)]
        got.append(lax.ppermute(sends[shift - 1], "chan", pairs))
    earlier = chan_range < me
    slot = jnp.minimum(jnp.sum(earlier & (owners == owners[me])), capacity - 1)
    picked = order[me * spread + spread_range]
    local = jnp.stack(
        [to_tiles(generator[0, 0], TS)[picked], to_tiles(hamiltonian[0, 0], TS)[picked]], axis=1
    ).reshape(2 * spread * TS, TS)
    got[0] = jnp.concatenate([local, cross_weights[0, 0][slot].reshape(-1, TS)], axis=0)
    got = jnp.stack(got)
    tiles_got = got[:, : 2 * spread * TS].reshape(channels, spread, 2, TS, TS)
    weights_cross = got[(me - owners[me]) % channels, 2 * spread * TS :].reshape(-1)

    mixer = recoupling[recoupling_index[me, 0]]
    column_of = (spread_range[None, :] * channels + source[:, None]).reshape(-1)
    mixer_in = mixer[:, column_of]
    cross = tiles_got.reshape(tile_count, 2, TS, TS)
    generator_mixed = jnp.einsum("ji,ixy->jxy", mixer_in, cross[:, 0], precision=highest)
    hamilton_mixed = jnp.einsum("ji,ixy->jxy", mixer_in, cross[:, 1], precision=highest)
    product = bracket(
        from_tiles(generator_mixed, TS), from_tiles(hamilton_mixed, TS), weights_cross
    )
    mixer_out = mixer[:, (spread_range[None, :] * channels + dest[:, None]).reshape(-1)]
    back = jnp.einsum("ji,jxy->ixy", mixer_out, to_tiles(product, TS), precision=highest)
    back = back.reshape(channels, spread, TS, TS)
    home = []
    for shift in range(1, channels):
        pairs = [(c, (c + shift) % channels) for c in range(channels)]
        home.append(lax.ppermute(back[shift], "chan", pairs))
    place = order[(source[:, None] * spread + spread_range[None, :]).reshape(-1)]
    kept = jnp.zeros((tile_count, TS, TS), jnp.float32).at[place[:spread]].set(back[0])
    kept = from_tiles(kept, TS)

    direct = bracket(generator[0, 0], hamiltonian[0, 0], pair_weights[0, 0])
    return finish(0.5 * (direct + direct.T + kept + kept.T), home, place[spread:])[None, None]


def solution(mesh):
    placed = (
        P(("groups", "chan"), ("tile", "rep"), None, None),
        P(("groups", "chan"), ("tile", "rep"), None, None),
        P(("groups", "chan"), ("tile", "rep"), None),
        P(("groups", "chan"), ("tile", "rep"), None, None),
        P(),
        P("groups", ("tile", "rep")),
        P(("groups", "chan"), ("tile", "rep"), None),
        P("groups", ("tile", "rep")),
    )
    return jax.shard_map(
        body,
        mesh=mesh,
        in_specs=placed,
        out_specs=P(("groups", "chan"), ("tile", "rep"), None, None),
        check_vma=False,
    )
```
